32 devices in a mesh: row: 4 (over z), col: 8 (over y, x, core).
Axes of the slice: x: 2, y: 2, z: 4, core: 2. Of those that a mesh axis runs over, the one named last changes fastest.
Arguments:
- precision_diag: float32 [32, 256, 256], P(('row', 'col')), may hold values from -0.1 to 4.6, as said below
- precision_pairs: float32 [32, 7, 256, 256], P(('row', 'col')), may hold values from -0.024 to 0.024
- pattern_cols: int32 [32, 7], P(('row', 'col')), may hold values from -1 to 31, as said below
- newton_diag: float32 [32, 256, 256], P(('row', 'col')), may hold values from -0.1 to 0.1, as said below
- newton_pairs: float32 [32, 7, 256, 256], P(('row', 'col')), may hold values from -0.006 to 0.006
- warm_start: float32 [32, 96, 256], P(('row', 'col')), may hold values from -15 to 15
- target_rows: int32 [96], replicated, may hold values from 0 to 8191, as said below
Outputs:
- inverse_panel: float32 [32, 96, 256], P(('row', 'col'))
- hessian_block: float32 [96, 96], P('row', 'col')
The draws below stay inside these ranges and needn't reach their ends.
Inputs may be any that keep to these rules, and one draw needn't show every extreme that they name: `pattern_cols`: each row lists its live entries first and -1 for the rest; it has 4 to 7 live entries, some row exactly 7 and some fewer. The live entries of block row I are distinct, differ from I, and lie in the group of 8 consecutive block rows that holds I (groups start at multiples of 8). `precision_diag`: each tile is symmetric, and X is positive definite. `newton_diag`: each tile is symmetric. `target_rows`: the 96 entries are distinct rows of X.
All inputs are finite; a program needn't handle non-finite values.
Results may differ from the reference program's by a relative error of at most 0.0003.
Values sent between devices are 32-bit elements; how exact they have to be, the bound alone decides.
No kernel may reach another device: no remote copies, remote signals or barrier semaphores. Data moves between devices by JAX's collectives and lax.ppermute only.
A program may use at most 64 MiB of HBM per device.

```python
import math
import jax
import jax.numpy as jnp
from jax import lax

B = 256
PAIR_CAP = 7
C = 96
NB = 32
GROUP_BLOCK_ROWS = 8


def symmetric_part(entries, scale):
    return (entries + jnp.swapaxes(entries, 1, 2)) * (scale / math.sqrt(2.0))


def draw_precision_diag(key, part):
    first_key, second_key = jax.random.split(jax.random.fold_in(key, 101))
    entries = jnp.clip(jax.random.normal(first_key, (NB, B, B), jnp.float32), -6.0, 6.0)
    diagonal_entries = jnp.exp(jax.random.uniform(second_key, (NB, B), jnp.float32, math.log(1.5), math.log(4.5)))
    identity = jnp.eye(B, dtype=jnp.float32)
    return symmetric_part(entries, 0.08 / math.sqrt(B)) + identity[None, :, :] * diagonal_entries[:, :, None]


def draw_newton_diag(key, part):
    first_key = jax.random.fold_in(jax.random.fold_in(key, 202), 0)
    entries = jnp.clip(jax.random.normal(first_key, (NB, B, B), jnp.float32), -6.0, 6.0)
    return symmetric_part(entries, 0.016 / math.sqrt(B))


def draw_warm_start(key, part):
    first_key, second_key = jax.random.split(jax.random.fold_in(key, 303))
    growth = 0.5 * 3.0 ** (jnp.arange(NB, dtype=jnp.float32) / NB)
    entries = jnp.clip(jax.random.normal(first_key, (NB, C, B), jnp.float32), -5.0, 5.0)
    rough = jnp.exp(jax.random.uniform(second_key, (NB, C, B), jnp.float32, math.log(0.5), math.log(2.0)))
    return entries * rough * growth[:, None, None]


def draw_pattern_cols(key, part):
    first_key, second_key, third_key = jax.random.split(jax.random.fold_in(key, 404), 3)
    row_index = jnp.arange(NB, dtype=jnp.int32)
    slot_location = row_index % GROUP_BLOCK_ROWS
    counts = jax.random.randint(first_key, (NB,), 4, PAIR_CAP + 1)
    counts = jnp.where(slot_location == 0, PAIR_CAP, counts)
    counts = jnp.where(slot_location == 1, 4, counts)
    hub_slots = jax.random.randint(second_key, (NB // GROUP_BLOCK_ROWS,), 0, GROUP_BLOCK_ROWS)
    hub_row = hub_slots[row_index // GROUP_BLOCK_ROWS]
    candidate_items = jnp.arange(GROUP_BLOCK_ROWS, dtype=jnp.int32)
    rank_scores = jax.random.randint(third_key, (NB, GROUP_BLOCK_ROWS), 0, 1 << 20) * GROUP_BLOCK_ROWS + candidate_items[None, :]
    rank_scores = jnp.where(candidate_items[None, :] == hub_row[:, None], rank_scores + (1 << 29), rank_scores)
    final_reward = (candidate_items[None, :] == GROUP_BLOCK_ROWS - 1) & (slot_location[:, None] == 0)
    rank_scores = jnp.where(final_reward, rank_scores + (1 << 28), rank_scores)
    rank_scores = jnp.where(candidate_items[None, :] == slot_location[:, None], -1, rank_scores)
    ranking = jnp.argsort(-rank_scores, axis=1, stable=True)[:, :PAIR_CAP]
    columns = (row_index - slot_location)[:, None] + ranking
    live_mask = jnp.arange(PAIR_CAP)[None, :] < counts[:, None]
    return jnp.where(live_mask, columns, -1).astype(jnp.int32)


def draw_target_rows(key, part):
    first_key, second_key = jax.random.split(jax.random.fold_in(key, 505))
    inner = jax.random.permutation(first_key, NB * B - 2)[:C - 2].astype(jnp.int32) + 1
    ends = jnp.array([0, NB * B - 1], dtype=jnp.int32)
    chosen = jnp.concatenate([ends, inner])
    return jax.random.permutation(second_key, chosen).astype(jnp.int32)


def levels(own_key, extent, pieces, low, largest):
    def one(dim, parts):
        draws = jax.random.uniform(jax.random.fold_in(jax.random.fold_in(own_key, 6), dim), (parts,), jnp.float32, low / len(pieces), largest / len(pieces))
        return jnp.repeat(jnp.exp(draws), extent[dim] // parts).reshape((-1,) + (1,) * (len(extent) - dim - 1))

    level = one(*pieces[0])
    for cut in pieces[1:]:
        level = level * one(*cut)
    return level


def normal_values(key, shape, width, most, cuts=(), kind=jnp.bfloat16):
    values = jax.random.normal(key, shape, jnp.float32) * width
    if len(cuts) > 0:
        values = levels(key, shape, cuts, -0.22, 0.18) * values
    return jnp.clip(values, min=-most, max=most).astype(kind)


def setup_inputs(seed: int = 0) -> dict:
    streams_of = jax.random.split(jax.random.key(seed), 8)
    precision_diag = draw_precision_diag(jax.random.fold_in(streams_of[7], 71), 0)
    precision_pairs = normal_values(streams_of[1], (NB, PAIR_CAP, B, B), (0.064 / B ** 0.5), 0.024, ((0, 32),), jnp.float32)
    pattern_cols = draw_pattern_cols(jax.random.fold_in(streams_of[7], 71), 0)
    newton_diag = draw_newton_diag(jax.random.fold_in(streams_of[7], 71), 0)
    newton_pairs = normal_values(streams_of[4], (NB, PAIR_CAP, B, B), (0.016 / B ** 0.5), 0.006, ((0, 32),), jnp.float32)
    warm_start = draw_warm_start(jax.random.fold_in(streams_of[7], 71), 0)
    target_rows = draw_target_rows(jax.random.fold_in(streams_of[7], 71), 0)
    return {"precision_diag": precision_diag, "precision_pairs": precision_pairs, "pattern_cols": pattern_cols, "newton_diag": newton_diag, "newton_pairs": newton_pairs, "warm_start": warm_start, "target_rows": target_rows}


HIGHEST = lax.Precision.HIGHEST


def apply_blocks(blocks, diag_tiles, pair_tiles, pattern_cols):
    live_mask = pattern_cols >= 0
    safe_cols = jnp.where(live_mask, pattern_cols, 0).astype(jnp.int32)
    weights = live_mask.astype(jnp.float32)[:, :, None, None]
    blocks = blocks.astype(jnp.float32)
    diag_tiles = diag_tiles.astype(jnp.float32)
    pair_tiles = pair_tiles.astype(jnp.float32)
    picked = blocks[safe_cols] * weights
    own_rows = jnp.einsum("icb,iab->ica", blocks, diag_tiles, precision=HIGHEST)
    own_rows = own_rows + jnp.einsum("ikcb,ikab->ica", picked, pair_tiles, precision=HIGHEST)
    moved_terms = jnp.einsum("icb,ikba->ikca", blocks, pair_tiles, precision=HIGHEST) * weights
    spread = jnp.zeros_like(blocks).at[safe_cols.reshape(-1)].add(moved_terms.reshape((-1,) + blocks.shape[1:]))
    return own_rows + spread


def column_dots(first, second):
    return jnp.sum(first * second, axis=(0, 2))


def reference(precision_diag, precision_pairs, pattern_cols, newton_diag, newton_pairs, warm_start, target_rows):
    global_rows = jnp.arange(NB * B, dtype=jnp.int32).reshape(NB, 1, B)
    unit_columns = (global_rows == target_rows[None, :, None]).astype(jnp.float32)
    solution = warm_start
    residual = unit_columns - apply_blocks(solution, precision_diag, precision_pairs, pattern_cols)
    norm_now = column_dots(residual, residual)
    direction = residual
    for iteration in range(2):
        images = apply_blocks(direction, precision_diag, precision_pairs, pattern_cols)
        step_size = norm_now / column_dots(direction, images)
        solution = solution + step_size[None, :, None] * direction
        if iteration == 0:
            residual = residual - step_size[None, :, None] * images
            norm_next = column_dots(residual, residual)
            direction = residual + (norm_next / norm_now)[None, :, None] * direction
            norm_now = norm_next
    newton_image = apply_blocks(solution, newton_diag, newton_pairs, pattern_cols)
    hessian = jnp.einsum("icb,idb->cd", solution, newton_image, precision=HIGHEST)
    return solution, hessian
```

```python
import functools

import jax
import jax.numpy as jnp
from jax import lax
from jax.experimental import pallas as pl
from jax.experimental.pallas import tpu as pltpu
from jax.sharding import Mesh, PartitionSpec as P

F32 = jnp.float32
BF16 = jnp.bfloat16
ALL = ("row", "chip", "core")
VMEM_LIMIT = 24 << 20
LANES = 128
HALF = 64

NT = (((1,), (1,)), ((), ()))
NN = (((1,), (0,)), ((), ()))


def split(value):
    high = value.astype(BF16)
    low = (value - high.astype(F32)).astype(BF16)
    return high, low


def dot3(left, right, dims):
    rows = left[0].shape[0]
    both = jnp.concatenate(left, axis=0)
    first = lax.dot_general(both, right[0], dims, preferred_element_type=F32)
    second = lax.dot_general(left[0], right[1], dims, preferred_element_type=F32)
    return first[:rows] + first[rows:] + second


def row_sums(product):
    ones = jnp.ones((8, product.shape[1]), F32)
    sums = lax.dot_general(
        ones, product, NT, precision=lax.Precision.HIGHEST, preferred_element_type=F32
    )
    return sums[0:1]


def column_of(row):
    n = row.shape[1]
    eye = lax.broadcasted_iota(jnp.int32, (n, n), 0) == lax.broadcasted_iota(
        jnp.int32, (n, n), 1
    )
    return jnp.sum(jnp.where(eye, row, 0.0), axis=1, keepdims=True)


def contributions(slots, core, tiles, panel, keep, send):
    keep[...] = jnp.zeros_like(keep)
    send[...] = jnp.zeros_like(send)
    for k in range(tiles.shape[0]):
        slot = slots[k]

        @pl.when(slot >= 0)
        def _():
            value = dot3(panel, split(tiles[k]), NN)
            chip = slot // 2

            @pl.when(slot % 2 == core)
            def _():
                keep[chip] = value

            @pl.when(slot % 2 != core)
            def _():
                send[chip] = value


def half_apply(slots, core, tiles, diag, panel, same, other, acc):
    acc[...] = dot3(panel, split(diag[...]), NT) * 0.5
    for k in range(tiles.shape[0]):
        slot = slots[k]

        @pl.when(slot >= 0)
        def _():
            chip = slot // 2
            picked = jnp.where(slot % 2 == core, same[chip], other[chip])
            acc[...] += dot3(split(picked), split(tiles[k]), NT)


def first_kernel(meta, tiles, panel, keep, send):
    contributions(meta, meta[tiles.shape[0]], tiles, split(panel[...]), keep, send)


def pack_kernel(panel, keep, received, out):
    value = panel[...]
    for chip in range(keep.shape[0]):
        out[0, chip] = value
        out[1, chip] = keep[chip] + received[chip]


def residual_kernel(
    meta, tiles, diag, panel, both, other, target, residual, keep, send, acc
):
    core = meta[tiles.shape[0]]
    parts = split(panel[...])
    half_apply(meta, core, tiles, diag, parts, both.at[0], other, acc)
    total = acc[...] + dot3(parts, split(diag[...]), NT) * 0.5
    for chip in range(both.shape[1]):
        total = total + both[1, chip]
    rows, size = panel.shape
    unit = target[...] == lax.broadcasted_iota(jnp.int32, (rows, size), 1)
    value = unit.astype(F32) - total
    residual[...] = value
    contributions(meta, core, tiles, split(value), keep, send)


def image_kernel(
    meta, tiles, diag, panel, both, other, image, half, sums
):
    core = meta[tiles.shape[0]]
    value = panel[...]
    parts = split(value)
    half_apply(meta, core, tiles, diag, parts, both.at[0], other, half)
    total = half[...] + dot3(parts, split(diag[...]), NT) * 0.5
    for chip in range(both.shape[1]):
        total = total + both[1, chip]
    image[...] = total
    sums[0:1] = row_sums(value * value)
    sums[1:2] = row_sums(value * total)
    sums[2:3] = row_sums(total * total)


def half_kernel(meta, tiles, diag, panel, both, other, out):
    half_apply(
        meta, meta[tiles.shape[0]], tiles, diag, split(panel[...]), both.at[0], other, out
    )


def all_half(slots, tiles, diag, panel, gathered, acc):
    acc[...] = dot3(panel, split(diag[...]), NT) * 0.5
    for k in range(tiles.shape[0]):
        slot = slots[k]

        @pl.when(slot >= 0)
        def _():
            acc[...] += dot3(split(gathered[slot]), split(tiles[k]), NT)


def middle_kernel(
    groups,
    parts_rows,
    parts_cols,
    meta,
    tiles,
    diag,
    newton_tiles,
    newton_diag,
    start,
    residual,
    image,
    gathered,
    half_residual,
    newton_start,
    newton_residual,
    sums,
    x_out,
    d_out,
    norm_out,
    packed,
    half_image,
    newton_image,
    left_pad,
    right_pad,
    blocks,
):
    image_parts = split(image[...])
    all_half(meta, tiles, diag, image_parts, gathered, half_image)
    all_half(meta, newton_tiles, newton_diag, image_parts, gathered, newton_image)
    totals = sums[0]
    for device in range(1, sums.shape[0]):
        totals = totals + sums[device]
    rr, rq, qq = totals[0:1], totals[1:2], totals[2:3]
    step = rr / rq
    norm = rr - 2.0 * step * rq + step * step * qq
    norm_out[...] = norm
    step_col = column_of(step)
    grow = 1.0 + column_of(norm / rr)
    r, q = residual[...], image[...]
    x1 = start[...] + step_col * r
    d1 = grow * r - step_col * q
    x_out[...] = x1
    d_out[...] = d1
    half_d = grow * half_residual[...] - step_col * half_image[...]
    curvature = 2.0 * row_sums(d1 * half_d)
    ux = newton_start[...] + step_col * newton_residual[...]
    ud = grow * newton_residual[...] - step_col * newton_image[...]
    rows = C = x1.shape[0]
    hr, hc = C // parts_rows, C // parts_cols
    total = None
    for side, (v, u) in enumerate(((x1, ux), (d1, ud))):
        left_pad[...] = jnp.zeros_like(left_pad)
        right_pad[...] = jnp.zeros_like(right_pad)
        for r_index in range(parts_rows):
            for kind, (v2, u2) in enumerate(((x1, ux), (d1, ud))):
                at = r_index * LANES + side * HALF + kind * hr
                left_pad[at : at + hr] = v2[r_index * hr : (r_index + 1) * hr]
                right_pad[at : at + hr] = u2[r_index * hr : (r_index + 1) * hr]
        term = dot3(split(v), split(right_pad[...]), NT) + dot3(
            split(u), split(left_pad[...]), NT
        )
        total = term if total is None else total + term
    blocks[...] = total
    for r_index in range(parts_rows):
        for c_index in range(parts_cols):
            at = r_index * parts_cols + c_index
            packed[at, 0:hc] = blocks[
                c_index * hc : (c_index + 1) * hc,
                r_index * LANES : (r_index + 1) * LANES,
            ]
            packed[at, hc : hc + 1, 0:C] = curvature
            packed[at, hc : hc + 1, C:LANES] = jnp.zeros((1, LANES - C), F32)


def last_kernel(parts_rows, parts_cols, meta, x1, d1, norm, received, x_out, hessian):
    total = received[0]
    for device in range(1, received.shape[0]):
        total = total + received[device]
    C = x1.shape[0]
    hr, hc = C // parts_rows, C // parts_cols
    step = norm[...] / total[hc : hc + 1, 0:C]
    step_col = column_of(step)
    x_out[...] = x1[...] + step_col * d1[...]
    row_at, col_at = meta[0] * hr, meta[1] * hc
    wanted = lax.broadcasted_iota(jnp.int32, (C, hr), 0) == row_at + lax.broadcasted_iota(
        jnp.int32, (C, hr), 1
    )
    of_rows = jnp.sum(jnp.where(wanted, step_col, 0.0), axis=0, keepdims=True)
    wanted = lax.broadcasted_iota(jnp.int32, (hc, C), 1) == col_at + lax.broadcasted_iota(
        jnp.int32, (hc, C), 0
    )
    of_cols = jnp.sum(jnp.where(wanted, step, 0.0), axis=1, keepdims=True)
    xx = total[0:hc, 0:hr]
    dx = total[0:hc, hr : 2 * hr]
    xd = total[0:hc, HALF : HALF + hr]
    dd = total[0:hc, HALF + hr : HALF + 2 * hr]
    hessian[...] = xx + of_rows * dx + of_cols * (xd + of_rows * dd)


def call(body, outs, scalars, arrays, scratch=(), flops=0):
    smem = pl.BlockSpec(memory_space=pltpu.SMEM)
    vmem = pl.BlockSpec(memory_space=pltpu.VMEM)
    shapes = [jax.ShapeDtypeStruct(s, F32) for s in outs]
    moved = sum(a.size * 4 for a in arrays)
    return pl.pallas_call(
        body,
        out_shape=shapes,
        in_specs=[smem] * len(scalars) + [vmem] * len(arrays),
        out_specs=[vmem] * len(shapes),
        scratch_shapes=[pltpu.VMEM(s, F32) for s in scratch],
        cost_estimate=pl.CostEstimate(
            flops=flops, bytes_accessed=moved, transcendentals=0
        ),
        compiler_params=pltpu.CompilerParams(vmem_limit_bytes=VMEM_LIMIT),
    )(*scalars, *arrays)


def on_device(
    precision_diag,
    precision_pairs,
    pattern_cols,
    newton_diag,
    newton_pairs,
    warm_start,
    target_rows,
):
    groups = lax.axis_size("row")
    chips = lax.axis_size("chip")
    columns = chips * 2
    devices = groups * columns
    row, chip, core = (lax.axis_index(a) for a in ALL)
    column = chip * 2 + core
    block = row * columns + column
    C, B = warm_start.shape[1:]
    slots = jnp.where(pattern_cols >= 0, pattern_cols - row * columns, -1)[0]
    meta = jnp.concatenate([slots, core[None].astype(jnp.int32)])
    place = jnp.concatenate([row[None], column[None]]).astype(jnp.int32)
    target = (target_rows - block * B).astype(jnp.int32)[:, None]
    tiles, diag = precision_pairs[0], precision_diag[0]
    ntiles, ndiag = newton_pairs[0], newton_diag[0]
    panel = (C, B)
    blocks = (chips, C, B)
    swap = [(0, 1), (1, 0)]
    unit = 2 * C * B * B * 3

    def exchange(value, keep, send):
        received = lax.ppermute(send, "core", swap)
        (packed,) = call(pack_kernel, [(2,) + blocks], [], [value, keep, received])
        both = lax.all_to_all(packed, "chip", 1, 1, tiled=True)
        other = lax.ppermute(both[0], "core", swap)
        return both, other

    start = warm_start[0]
    keep, send = call(
        first_kernel, [blocks, blocks], [meta], [tiles, start], flops=7 * unit
    )
    both_start, other_start = exchange(start, keep, send)
    residual, keep, send = call(
        residual_kernel,
        [panel, blocks, blocks],
        [meta],
        [tiles, diag, start, both_start, other_start, target],
        scratch=[panel],
        flops=15 * unit,
    )
    both_residual, other_residual = exchange(residual, keep, send)
    image, half_residual, sums = call(
        image_kernel,
        [panel, panel, (3, C)],
        [meta],
        [tiles, diag, residual, both_residual, other_residual],
        flops=8 * unit,
    )
    (newton_start,) = call(
        half_kernel,
        [panel],
        [meta],
        [ntiles, ndiag, start, both_start, other_start],
        flops=8 * unit,
    )
    (newton_residual,) = call(
        half_kernel,
        [panel],
        [meta],
        [ntiles, ndiag, residual, both_residual, other_residual],
        flops=8 * unit,
    )
    all_sums = lax.all_to_all(
        jnp.broadcast_to(sums[None], (devices,) + sums.shape), ALL, 0, 0, tiled=True
    )
    gathered = lax.all_gather(image, ("chip", "core"), axis=0, tiled=False)
    hc = C // columns
    depth = -(-(hc + 1) // 8) * 8
    x1, d1, norm, packed = call(
        functools.partial(middle_kernel, chips, groups, columns),
        [panel, panel, (1, C), (devices, depth, LANES)],
        [meta],
        [
            tiles,
            diag,
            ntiles,
            ndiag,
            start,
            residual,
            image,
            gathered,
            half_residual,
            newton_start,
            newton_residual,
            all_sums,
        ],
        scratch=[
            panel,
            panel,
            (groups * LANES, B),
            (groups * LANES, B),
            (C, groups * LANES),
        ],
        flops=20 * unit,
    )
    received = lax.all_to_all(packed, ALL, 0, 0, tiled=True)
    solved, hessian = call(
        functools.partial(last_kernel, groups, columns),
        [panel, (hc, C // groups)],
        [place],
        [x1, d1, norm, received],
        flops=unit // 100,
    )
    return solved[None], hessian.T


def solution(mesh):
    rows, columns = mesh.devices.shape
    fine = Mesh(mesh.devices.reshape(rows, columns // 2, 2), ALL)
    placed = (
        P(ALL, None, None),
        P(ALL, None, None, None),
        P(ALL, None),
        P(ALL, None, None),
        P(ALL, None, None, None),
        P(ALL, None, None),
        P(),
    )
    return jax.shard_map(
        on_device,
        mesh=fine,
        in_specs=placed,
        out_specs=(P(ALL, None, None), P("row", ("chip", "core"))),
        check_vma=False,
    )
```

```python
import functools

import jax
import jax.numpy as jnp
from jax import lax
from jax.experimental import pallas as pl
from jax.experimental.pallas import tpu as pltpu
from jax.sharding import Mesh, PartitionSpec as P

F32 = jnp.float32
BF16 = jnp.bfloat16
ALL = ("row", "chip", "core")
GRANT = 24 << 20
LANES = 128
HALF = 64

NT = (((1,), (1,)), ((), ()))
NN = (((1,), (0,)), ((), ()))


def split(value):
    high = value.astype(BF16)
    low = (value - high.astype(F32)).astype(BF16)
    return high, low


def dot3(left, right, dims):
    rows = left[0].shape[0]
    both = jnp.concatenate(left, axis=0)
    first = lax.dot_general(both, right[0], dims, preferred_element_type=F32)
    second = lax.dot_general(left[0], right[1], dims, preferred_element_type=F32)
    return first[:rows] + first[rows:] + second


def dot_full(left, right, dims):
    return lax.dot_general(
        left, right, dims, precision=lax.Precision.HIGHEST, preferred_element_type=F32
    )


def row_sums(product):
    return dot_full(jnp.ones((8, product.shape[1]), F32), product, NT)[0:1]


def column_of(row):
    n = row.shape[1]
    eye = lax.broadcasted_iota(jnp.int32, (n, n), 0) == lax.broadcasted_iota(
        jnp.int32, (n, n), 1
    )
    return jnp.sum(jnp.where(eye, row, 0.0), axis=1, keepdims=True)


class Far:
    def __init__(self, array):
        self.array = array


class Fetched:
    def __init__(self, copies, ref):
        self.copies, self.ref, self.shape = copies, ref, ref.shape

    def wait(self, piece=None):
        for k in range(len(self.copies)) if piece is None else (piece,):
            if self.copies[k] is not None:
                self.copies[k].wait()
                self.copies[k] = None
        return self.ref

    def all(self):
        return self.wait()[...]

    def piece(self, k):
        return self.wait(k)[k]


def call(body, outs, scalars, groups, scratch=(), flops=0):
    flat, plan = [], []
    for group in groups:
        if isinstance(group, Far):
            group = pltpu.with_memory_space_constraint(group.array, pltpu.HBM)
        if isinstance(group, (tuple, list)):
            shape, pieces = (len(group),) + group[0].shape, len(group)
            plan.append((shape, pieces, len(flat), True))
            flat.extend(group)
        else:
            pieces = group.shape[0] if group.ndim == 3 else 1
            plan.append((group.shape, pieces, len(flat), False))
            flat.append(group)
    n_out, n_scratch = len(outs), len(scratch)

    def kernel(*refs):
        smem, refs = refs[: len(scalars)], refs[len(scalars) :]
        arrays, refs = refs[: len(flat)], refs[len(flat) :]
        out, refs = refs[:n_out], refs[n_out:]
        mine, refs = refs[:n_scratch], refs[n_scratch:]
        buffers, sems = refs[: len(plan)], refs[len(plan)]
        fetched, at = [], 0
        for (shape, pieces, first, stacked), buffer in zip(plan, buffers):
            copies = []
            for k in range(pieces):
                if stacked:
                    source, target = arrays[first + k], buffer.at[k]
                elif len(shape) == 3:
                    source, target = arrays[first].at[k], buffer.at[k]
                else:
                    source, target = arrays[first], buffer
                copy = pltpu.make_async_copy(source, target, sems.at[at])
                copy.start()
                copies.append(copy)
                at += 1
            fetched.append(Fetched(copies, buffer))
        body(*smem, *fetched, *out, *mine)
        for one in fetched:
            one.wait()

    smem = pl.BlockSpec(memory_space=pltpu.SMEM)
    vmem = pl.BlockSpec(memory_space=pltpu.VMEM)
    shapes = [jax.ShapeDtypeStruct(s, F32) for s in outs]
    total = sum(p[1] for p in plan)
    return pl.pallas_call(
        kernel,
        out_shape=shapes,
        in_specs=[smem] * len(scalars) + [pl.BlockSpec(memory_space=pl.ANY)] * len(flat),
        out_specs=[vmem] * len(shapes),
        scratch_shapes=[pltpu.VMEM(s, F32) for s in scratch]
        + [pltpu.VMEM(p[0], flat[p[2]].dtype) for p in plan]
        + [pltpu.SemaphoreType.DMA((total,))],
        cost_estimate=pl.CostEstimate(
            flops=flops,
            bytes_accessed=sum(a.size * 4 for a in flat),
            transcendentals=0,
        ),
        compiler_params=pltpu.CompilerParams(vmem_limit_bytes=GRANT),
    )(*scalars, *flat)


class Way:
    def __init__(self, chips):
        self.chips, self.power = chips, chips & (chips - 1) == 0

    def pairs(self, k):
        n = self.chips
        return [(i, i ^ k if self.power else (i + k) % n) for i in range(n)]

    def to(self, here, there):
        n = self.chips
        return there ^ here if self.power else lax.rem(there - here + n, n)

    def source(self, k):
        return k if self.power else (self.chips - k) % self.chips


def contributions(way, slots, chip, core, tiles, panel, keep, send):
    keep[...] = jnp.zeros_like(keep)
    send[...] = jnp.zeros_like(send)
    for k in range(tiles.shape[0]):
        slot = slots[k]
        tiles.wait(k)

        @pl.when(slot >= 0)
        def _():
            value = dot3(panel, split(tiles.ref[k]), NN)
            place = way.to(chip, slot // 2)

            @pl.when(slot % 2 == core)
            def _():
                keep[place] = value

            @pl.when(slot % 2 != core)
            def _():
                send[place] = value


def off_diagonal(way, slots, chip, core, tiles, same, other, acc, dot):
    same.wait()
    other.wait()
    for k in range(tiles.shape[0]):
        slot = slots[k]
        tiles.wait(k)

        @pl.when(slot >= 0)
        def _():
            place = way.to(chip, slot // 2)
            picked = jnp.where(slot % 2 == core, same.ref[place], other.ref[place])
            acc[...] += dot(picked, tiles.ref[k], NT)


def quick(left, right, dims):
    return dot3(split(left), split(right), dims)


def first_kernel(way, meta, panel, tiles, keep, send):
    n = tiles.shape[0]
    contributions(
        way, meta, meta[n], meta[n + 1], tiles, split(panel.all()), keep, send
    )


def sum_kernel(keep, received, *outs):
    for k, out in enumerate(outs):
        out[...] = keep.piece(k) + received.piece(k)


def diag_kernel(panel, diag, newton_diag, image, newton):
    value = panel.all()
    image[...] = dot_full(value, diag.all(), NT)
    newton[...] = 0.5 * dot_full(value, newton_diag.all(), NT)


def residual_kernel(
    way, meta, base, target, same, other, added, tiles, residual, keep, send
):
    n = tiles.shape[0]
    chip, core = meta[n], meta[n + 1]
    residual[...] = base.all()
    off_diagonal(way, meta, chip, core, tiles, same, other, residual, quick)
    total = residual[...]
    for k in range(added.shape[0]):
        total = total + added.piece(k)
    rows, size = residual.shape
    unit = target.all() == lax.broadcasted_iota(jnp.int32, (rows, size), 1)
    value = unit.astype(F32) - total
    residual[...] = value
    contributions(way, meta, chip, core, tiles, split(value), keep, send)


def image_kernel(way, meta, panel, base, same, other, added, tiles, image, half, sums):
    n = tiles.shape[0]
    diag = base.all()
    half[...] = 0.5 * diag
    off_diagonal(way, meta, meta[n], meta[n + 1], tiles, same, other, half, quick)
    total = half[...] + 0.5 * diag
    for k in range(added.shape[0]):
        total = total + added.piece(k)
    image[...] = total
    value = panel.all()
    sums[0:1] = row_sums(value * value)
    sums[1:2] = row_sums(value * total)
    sums[2:3] = row_sums(total * total)


def half_kernel(way, meta, base, same, other, tiles, out):
    n = tiles.shape[0]
    out[...] = base.all()
    off_diagonal(way, meta, meta[n], meta[n + 1], tiles, same, other, out, dot_full)


def middle_kernel(
    way,
    parts_rows,
    parts_cols,
    meta,
    sums,
    start,
    residual,
    half_residual,
    newton_start,
    newton_residual,
    base,
    newton_base,
    same,
    other,
    tiles,
    newton_tiles,
    x_out,
    d_out,
    norm_out,
    keep,
    send,
    packed,
    half_image,
    newton_image,
    left_pad,
    right_pad,
    blocks,
):
    n = tiles.shape[0]
    chip, core = meta[n], meta[n + 1]
    half_image[...] = 0.5 * base.all()
    off_diagonal(way, meta, chip, core, tiles, same, other, half_image, quick)
    newton_image[...] = newton_base.all()
    off_diagonal(
        way, meta, chip, core, newton_tiles, same, other, newton_image, dot_full
    )
    sums.wait()
    totals = sums.ref[0]
    for device in range(1, sums.shape[0]):
        totals = totals + sums.ref[device]
    rr, rq, qq = totals[0:1], totals[1:2], totals[2:3]
    step = rr / rq
    norm = rr - 2.0 * step * rq + step * step * qq
    norm_out[...] = norm
    step_col = column_of(step)
    grow = 1.0 + column_of(norm / rr)
    r, q = residual.all(), same.ref[0]
    x1 = start.all() + step_col * r
    d1 = grow * r - step_col * q
    x_out[...] = x1
    d_out[...] = d1
    half_d = grow * half_residual.all() - step_col * half_image[...]
    curvature = 2.0 * row_sums(d1 * half_d)
    ux = newton_start.all() + step_col * newton_residual.all()
    ud = grow * newton_residual.all() - step_col * newton_image[...]
    count = x1.shape[0]
    hr, hc = count // parts_rows, count // parts_cols
    total = None
    for side, (v, u) in enumerate(((x1, ux), (d1, ud))):
        left_pad[...] = jnp.zeros_like(left_pad)
        right_pad[...] = jnp.zeros_like(right_pad)
        for r_index in range(parts_rows):
            for kind, (v2, u2) in enumerate(((x1, ux), (d1, ud))):
                at = r_index * LANES + side * HALF + kind * hr
                left_pad[at : at + hr] = v2[r_index * hr : (r_index + 1) * hr]
                right_pad[at : at + hr] = u2[r_index * hr : (r_index + 1) * hr]
        term = dot_full(v, right_pad[...], NT) + dot_full(u, left_pad[...], NT)
        total = term if total is None else total + term
    blocks[...] = total
    for r_index in range(parts_rows):
        for c_index in range(parts_cols):
            piece = blocks[
                c_index * hc : (c_index + 1) * hc,
                r_index * LANES : (r_index + 1) * LANES,
            ]
            lanes = slice(r_index * LANES, (r_index + 1) * LANES)
            at = r_index * (parts_cols // 2) + c_index // 2
            target = packed.at[c_index % 2, at]
            target[0:hc] = piece
            target[hc : hc + 1, 0:count] = curvature
            target[hc : hc + 1, count:LANES] = jnp.zeros((1, LANES - count), F32)
    keep[...] = packed[core]
    send[...] = packed[1 - core]


def add_kernel(first, second, out):
    out[...] = first.all() + second.all()


def last_kernel(parts_rows, parts_cols, meta, received, norm, x1, d1, x_out, hessian):
    received.wait()
    total = received.ref[0]
    for device in range(1, received.shape[0]):
        total = total + received.ref[device]
    count = x1.shape[0]
    hr, hc = count // parts_rows, count // parts_cols
    step = norm.all() / total[hc : hc + 1, 0:count]
    step_col = column_of(step)
    x_out[...] = x1.all() + step_col * d1.all()
    row_at, col_at = meta[0] * hr, meta[1] * hc
    wanted = lax.broadcasted_iota(jnp.int32, (count, hr), 0) == row_at + (
        lax.broadcasted_iota(jnp.int32, (count, hr), 1)
    )
    of_rows = jnp.sum(jnp.where(wanted, step_col, 0.0), axis=0, keepdims=True)
    wanted = lax.broadcasted_iota(jnp.int32, (hc, count), 1) == col_at + (
        lax.broadcasted_iota(jnp.int32, (hc, count), 0)
    )
    of_cols = jnp.sum(jnp.where(wanted, step, 0.0), axis=1, keepdims=True)
    xx = total[0:hc, 0:hr]
    dx = total[0:hc, hr : 2 * hr]
    xd = total[0:hc, HALF : HALF + hr]
    dd = total[0:hc, HALF + hr : HALF + 2 * hr]
    hessian[...] = xx + of_rows * dx + of_cols * (xd + of_rows * dd)


def on_device(
    precision_diag,
    precision_pairs,
    pattern_cols,
    newton_diag,
    newton_pairs,
    warm_start,
    target_rows,
):
    groups = lax.axis_size("row")
    chips = lax.axis_size("chip")
    columns = chips * 2
    devices = groups * columns
    row, chip, core = (lax.axis_index(a).astype(jnp.int32) for a in ALL)
    column = chip * 2 + core
    block = row * columns + column
    count, size = warm_start.shape[1:]
    slots = jnp.where(pattern_cols >= 0, pattern_cols - row * columns, -1)[0]
    meta = jnp.concatenate([slots, chip[None], core[None]])
    place = jnp.concatenate([row[None], column[None]])
    target = (target_rows - block * size).astype(jnp.int32)[:, None]
    tiles, diag = Far(precision_pairs[0]), Far(precision_diag[0])
    ntiles, ndiag = Far(newton_pairs[0]), Far(newton_diag[0])
    panel = (count, size)
    stack = (chips, count, size)
    swap = [(0, 1), (1, 0)]
    way = Way(chips)
    unit = 2 * count * size * size * 3
    n = precision_pairs.shape[1]

    def gather(value):
        same, other = [value] + [None] * (chips - 1), [None] * chips
        for k in range(1, chips):
            same[way.source(k)] = lax.ppermute(value, "chip", way.pairs(k))
        for k in range(chips):
            other[k] = lax.ppermute(same[k], "core", swap)
        return same, other

    def scatter(keep, send):
        received = lax.ppermute(send, "core", swap)
        sums = call(sum_kernel, [panel] * chips, [], [keep, received])
        return [sums[0]] + [
            lax.ppermute(sums[k], "chip", way.pairs(k)) for k in range(1, chips)
        ]

    def diagonal(value):
        return call(
            diag_kernel, [panel, panel], [], [value, diag, ndiag], flops=4 * unit
        )

    start = warm_start[0]
    same0, other0 = gather(start)
    keep, send = call(
        functools.partial(first_kernel, way),
        [stack, stack],
        [meta],
        [start, tiles],
        flops=n * unit,
    )
    added = scatter(keep, send)
    base0, nbase0 = diagonal(start)
    residual, keep, send = call(
        functools.partial(residual_kernel, way),
        [panel, stack, stack],
        [meta],
        [base0, target, same0, other0, added, tiles],
        flops=2 * n * unit,
    )
    same1, other1 = gather(residual)
    added = scatter(keep, send)
    base1, nbase1 = diagonal(residual)
    (newton_start,) = call(
        functools.partial(half_kernel, way),
        [panel],
        [meta],
        [nbase0, same0, other0, ntiles],
        flops=2 * n * unit,
    )
    image, half_residual, sums = call(
        functools.partial(image_kernel, way),
        [panel, panel, (3, count)],
        [meta],
        [residual, base1, same1, other1, added, tiles],
        flops=n * unit,
    )
    same2, other2 = gather(image)
    all_sums = lax.all_to_all(
        jnp.broadcast_to(sums[None], (devices,) + sums.shape), ALL, 0, 0, tiled=True
    )
    base2, nbase2 = diagonal(image)
    (newton_residual,) = call(
        functools.partial(half_kernel, way),
        [panel],
        [meta],
        [nbase1, same1, other1, ntiles],
        flops=2 * n * unit,
    )
    hc = count // columns
    depth = -(-(hc + 1) // 8) * 8
    share = (devices // 2, depth, LANES)
    x1, d1, norm, keep, send = call(
        functools.partial(middle_kernel, way, groups, columns),
        [panel, panel, (1, count), share, share],
        [meta],
        [
            all_sums,
            start,
            residual,
            half_residual,
            newton_start,
            newton_residual,
            base2,
            nbase2,
            same2,
            other2,
            tiles,
            ntiles,
        ],
        scratch=[
            (2,) + share,
            panel,
            panel,
            (groups * LANES, size),
            (groups * LANES, size),
            (count, groups * LANES),
        ],
        flops=4 * n * unit,
    )
    received = lax.ppermute(send, "core", swap)
    (share_sum,) = call(add_kernel, [share], [], [keep, received])
    received = lax.all_to_all(share_sum, ("row", "chip"), 0, 0, tiled=True)
    solved, hessian = call(
        functools.partial(last_kernel, groups, columns),
        [panel, (hc, count // groups)],
        [place],
        [received, norm, x1, d1],
        flops=unit // 100,
    )
    return solved[None], hessian.T


def solution(mesh):
    rows, columns = mesh.devices.shape
    fine = Mesh(mesh.devices.reshape(rows, columns // 2, 2), ALL)
    placed = (
        P(ALL, None, None),
        P(ALL, None, None, None),
        P(ALL, None),
        P(ALL, None, None),
        P(ALL, None, None, None),
        P(ALL, None, None),
        P(),
    )
    return jax.shard_map(
        on_device,
        mesh=fine,
        in_specs=placed,
        out_specs=(P(ALL, None, None), P("row", ("chip", "core"))),
        check_vma=False,
    )
```

```python
import functools

import jax
import jax.numpy as jnp
from jax import lax
from jax.experimental import pallas as pl
from jax.experimental.pallas import tpu as pltpu
from jax.sharding import Mesh, PartitionSpec as P

F32 = jnp.float32
BF16 = jnp.bfloat16
ALL = ("row", "chip", "core")
GRANT = 24 << 20
LANES = 128
HALF = 64

NT = (((1,), (1,)), ((), ()))
NN = (((1,), (0,)), ((), ()))


def split(value):
    high = value.astype(BF16)
    low = (value - high.astype(F32)).astype(BF16)
    return high, low


def dot3(left, right, dims):
    rows = left[0].shape[0]
    both = jnp.concatenate(left, axis=0)
    first = lax.dot_general(both, right[0], dims, preferred_element_type=F32)
    second = lax.dot_general(left[0], right[1], dims, preferred_element_type=F32)
    return first[:rows] + first[rows:] + second


def dot_full(left, right, dims):
    return lax.dot_general(
        left, right, dims, precision=lax.Precision.HIGHEST, preferred_element_type=F32
    )


def row_sums(product):
    return dot_full(jnp.ones((8, product.shape[1]), F32), product, NT)[0:1]


def column_of(row):
    n = row.shape[1]
    eye = lax.broadcasted_iota(jnp.int32, (n, n), 0) == lax.broadcasted_iota(
        jnp.int32, (n, n), 1
    )
    return jnp.sum(jnp.where(eye, row, 0.0), axis=1, keepdims=True)


class Far:
    def __init__(self, array):
        self.array = array


class Fetched:
    def __init__(self, copies, ref):
        self.copies, self.ref, self.shape = copies, ref, ref.shape

    def wait(self, piece=None):
        for k in range(len(self.copies)) if piece is None else (piece,):
            if self.copies[k] is not None:
                self.copies[k].wait()
                self.copies[k] = None
        return self.ref

    def all(self):
        return self.wait()[...]

    def piece(self, k):
        return self.wait(k)[k]


def call(body, outs, scalars, groups, scratch=(), flops=0):
    flat, plan = [], []
    for group in groups:
        if isinstance(group, Far):
            group = pltpu.with_memory_space_constraint(group.array, pltpu.HBM)
        if isinstance(group, (tuple, list)):
            shape, pieces = (len(group),) + group[0].shape, len(group)
            plan.append((shape, pieces, len(flat), True))
            flat.extend(group)
        else:
            pieces = group.shape[0] if group.ndim == 3 else 1
            plan.append((group.shape, pieces, len(flat), False))
            flat.append(group)
    n_out, n_scratch = len(outs), len(scratch)

    def kernel(*refs):
        smem, refs = refs[: len(scalars)], refs[len(scalars) :]
        arrays, refs = refs[: len(flat)], refs[len(flat) :]
        out, refs = refs[:n_out], refs[n_out:]
        mine, refs = refs[:n_scratch], refs[n_scratch:]
        buffers, sems = refs[: len(plan)], refs[len(plan)]
        fetched, at = [], 0
        for (shape, pieces, first, stacked), buffer in zip(plan, buffers):
            copies = []
            for k in range(pieces):
                if stacked:
                    source, target = arrays[first + k], buffer.at[k]
                elif len(shape) == 3:
                    source, target = arrays[first].at[k], buffer.at[k]
                else:
                    source, target = arrays[first], buffer
                copy = pltpu.make_async_copy(source, target, sems.at[at])
                copy.start()
                copies.append(copy)
                at += 1
            fetched.append(Fetched(copies, buffer))
        body(*smem, *fetched, *out, *mine)
        for one in fetched:
            one.wait()

    smem = pl.BlockSpec(memory_space=pltpu.SMEM)
    vmem = pl.BlockSpec(memory_space=pltpu.VMEM)
    shapes = [jax.ShapeDtypeStruct(s, F32) for s in outs]
    total = sum(p[1] for p in plan)
    return pl.pallas_call(
        kernel,
        out_shape=shapes,
        in_specs=[smem] * len(scalars) + [pl.BlockSpec(memory_space=pl.ANY)] * len(flat),
        out_specs=[vmem] * len(shapes),
        scratch_shapes=[pltpu.VMEM(s, F32) for s in scratch]
        + [pltpu.VMEM(p[0], flat[p[2]].dtype) for p in plan]
        + [pltpu.SemaphoreType.DMA((total,))],
        cost_estimate=pl.CostEstimate(
            flops=flops,
            bytes_accessed=sum(a.size * 4 for a in flat),
            transcendentals=0,
        ),
        compiler_params=pltpu.CompilerParams(vmem_limit_bytes=GRANT),
    )(*scalars, *flat)


class Way:
    def __init__(self, chips):
        self.chips, self.power = chips, chips & (chips - 1) == 0

    def pairs(self, k):
        n = self.chips
        return [(i, i ^ k if self.power else (i + k) % n) for i in range(n)]

    def to(self, here, there):
        n = self.chips
        return there ^ here if self.power else lax.rem(there - here + n, n)

    def source(self, k):
        return k if self.power else (self.chips - k) % self.chips


def seats(way, meta, tiles):
    n = tiles.shape[0]
    chip, core = meta[n], meta[n + 1]
    found = []
    for k in range(n):
        live = meta[k] >= 0
        slot = jnp.maximum(meta[k], 0)
        kind = jnp.where(slot % 2 == core, 0, way.chips)
        found.append((live, kind + way.to(chip, slot // 2)))
    return found


def contributions(way, meta, tiles, panel, work, keep, send):
    chips = way.chips
    work[0 : 2 * chips] = jnp.zeros((2 * chips,) + work.shape[1:], F32)
    for k, (live, seat) in enumerate(seats(way, meta, tiles)):
        value = dot3(panel, split(tiles.piece(k)), NN)
        work[jnp.where(live, seat, 2 * chips)] = value
    keep[...] = work[0:chips]
    send[...] = work[chips : 2 * chips]


def off_diagonal(way, meta, tiles, gathered, dot):
    gathered.wait()
    total = None
    for k, (live, seat) in enumerate(seats(way, meta, tiles)):
        picked = jnp.where(live, gathered.ref[seat], 0.0)
        term = dot(picked, tiles.piece(k), NT)
        total = term if total is None else total + term
    return total


def quick(left, right, dims):
    return dot3(split(left), split(right), dims)


def first_kernel(way, meta, panel, tiles, keep, send, work):
    contributions(way, meta, tiles, split(panel.all()), work, keep, send)


def diag_kernel(panel, diag, newton_diag, image, newton):
    value = panel.all()
    image[...] = dot_full(value, diag.all(), NT)
    newton[...] = 0.5 * dot_full(value, newton_diag.all(), NT)


def diag_half_kernel(
    way, meta, panel, diag, newton_diag, base, gathered, newton_tiles, image, newton, half
):
    diag_kernel(panel, diag, newton_diag, image, newton)
    half[...] = base.all() + off_diagonal(way, meta, newton_tiles, gathered, dot_full)


def residual_kernel(
    way, meta, base, target, gathered, tiles, added, residual, keep, send, work
):
    total = base.all() + off_diagonal(way, meta, tiles, gathered, quick)
    for k in range(added.shape[0]):
        total = total + added.piece(k)
    rows, size = residual.shape
    unit = target.all() == lax.broadcasted_iota(jnp.int32, (rows, size), 1)
    value = unit.astype(F32) - total
    residual[...] = value
    contributions(way, meta, tiles, split(value), work, keep, send)


def image_kernel(way, meta, panel, base, gathered, tiles, added, image, half, sums):
    off = off_diagonal(way, meta, tiles, gathered, quick)
    diag = base.all()
    half[...] = off + 0.5 * diag
    total = off + diag
    for k in range(added.shape[0]):
        total = total + added.piece(k)
    image[...] = total
    value = panel.all()
    sums[0:1] = row_sums(value * value)
    sums[1:2] = row_sums(value * total)
    sums[2:3] = row_sums(total * total)


def middle_kernel(
    way,
    parts_rows,
    parts_cols,
    meta,
    gathered,
    tiles,
    newton_tiles,
    base,
    newton_base,
    sums,
    start,
    residual,
    half_residual,
    newton_start,
    newton_residual,
    x_out,
    d_out,
    norm_out,
    keep,
    send,
    packed,
    order,
    blocks,
    pieces,
):
    core = meta[tiles.shape[0] + 1]
    half_image = 0.5 * base.all() + off_diagonal(way, meta, tiles, gathered, quick)
    newton_image = newton_base.all() + off_diagonal(
        way, meta, newton_tiles, gathered, quick
    )
    sums.wait()
    totals = sums.ref[0]
    for device in range(1, sums.shape[0]):
        totals = totals + sums.ref[device]
    rr, rq, qq = totals[0:1], totals[1:2], totals[2:3]
    step = rr / rq
    norm = rr - 2.0 * step * rq + step * step * qq
    norm_out[...] = norm
    step_col = column_of(step)
    grow = 1.0 + column_of(norm / rr)
    r, q = residual.all(), gathered.ref[0]
    x1 = start.all() + step_col * r
    d1 = grow * r - step_col * q
    x_out[...] = x1
    d_out[...] = d1
    half_d = grow * half_residual.all() - step_col * half_image
    curvature = 2.0 * row_sums(d1 * half_d)
    ux = newton_start.all() + step_col * newton_residual.all()
    ud = grow * newton_residual.all() - step_col * newton_image
    count = x1.shape[0]
    hr, hc = count // parts_rows, count // parts_cols
    for r_index in range(parts_rows):
        for kind, pair in enumerate(((x1, ux), (d1, ud))):
            at = (2 * r_index + kind) * hr
            for side in range(2):
                order[side, at : at + hr] = pair[side][
                    r_index * hr : (r_index + 1) * hr
                ]
    blocks[...] = dot_full(
        jnp.concatenate([x1, d1], axis=0), order[1], NT
    ) + dot_full(jnp.concatenate([ux, ud], axis=0), order[0], NT)
    for r_index in range(parts_rows):
        lanes = slice(2 * r_index * hr, 2 * (r_index + 1) * hr)
        pieces[:, 0 : 2 * hr] = blocks[0:count, lanes]
        pieces[:, HALF : HALF + 2 * hr] = blocks[count : 2 * count, lanes]
        for c_index in range(parts_cols):
            at = r_index * (parts_cols // 2) + c_index // 2
            target = packed.at[c_index % 2, at]
            target[0:hc] = pieces[c_index * hc : (c_index + 1) * hc]
            target[hc : hc + 1, 0:count] = curvature
    keep[...] = packed[core]
    send[...] = packed[1 - core]


def last_kernel(parts_rows, parts_cols, meta, received, norm, x1, d1, x_out, hessian):
    received.wait()
    total = received.ref[0]
    for device in range(1, received.shape[0]):
        total = total + received.ref[device]
    count = x1.shape[0]
    hr, hc = count // parts_rows, count // parts_cols
    step = norm.all() / total[hc : hc + 1, 0:count]
    step_col = column_of(step)
    x_out[...] = x1.all() + step_col * d1.all()
    row_at, col_at = meta[0] * hr, meta[1] * hc
    wanted = lax.broadcasted_iota(jnp.int32, (count, hr), 0) == row_at + (
        lax.broadcasted_iota(jnp.int32, (count, hr), 1)
    )
    of_rows = jnp.sum(jnp.where(wanted, step_col, 0.0), axis=0, keepdims=True)
    wanted = lax.broadcasted_iota(jnp.int32, (hc, count), 1) == col_at + (
        lax.broadcasted_iota(jnp.int32, (hc, count), 0)
    )
    of_cols = jnp.sum(jnp.where(wanted, step, 0.0), axis=1, keepdims=True)
    xx = total[0:hc, 0:hr]
    dx = total[0:hc, hr : 2 * hr]
    xd = total[0:hc, HALF : HALF + hr]
    dd = total[0:hc, HALF + hr : HALF + 2 * hr]
    hessian[...] = xx + of_rows * dx + of_cols * (xd + of_rows * dd)


def on_device(
    precision_diag,
    precision_pairs,
    pattern_cols,
    newton_diag,
    newton_pairs,
    warm_start,
    target_rows,
):
    groups = lax.axis_size("row")
    chips = lax.axis_size("chip")
    columns = chips * 2
    devices = groups * columns
    row, chip, core = (lax.axis_index(a).astype(jnp.int32) for a in ALL)
    column = chip * 2 + core
    block = row * columns + column
    count, size = warm_start.shape[1:]
    slots = jnp.where(pattern_cols >= 0, pattern_cols - row * columns, -1)[0]
    meta = jnp.concatenate([slots, chip[None], core[None]])
    place = jnp.concatenate([row[None], column[None]])
    target = (target_rows - block * size).astype(jnp.int32)[:, None]
    tiles, diag = Far(precision_pairs[0]), Far(precision_diag[0])
    ntiles, ndiag = Far(newton_pairs[0]), Far(newton_diag[0])
    panel = (count, size)
    stack = (chips, count, size)
    swap = [(0, 1), (1, 0)]
    way = Way(chips)
    unit = 2 * count * size * size * 3
    n = precision_pairs.shape[1]

    def gather(value):
        same = [value] + [None] * (chips - 1)
        for k in range(1, chips):
            same[way.source(k)] = lax.ppermute(value, "chip", way.pairs(k))
        return same

    def forward(same, after=None):
        other = []
        for block in same:
            if after is not None:
                block, _ = lax.optimization_barrier((block, after))
            other.append(lax.ppermute(block, "core", swap))
        return list(same) + other

    def scatter(keep, send):
        received = lax.ppermute(send, "core", swap)
        sums = [keep[k] + received[k] for k in range(chips)]
        return sums[-1], [sums[0]] + [
            lax.ppermute(sums[k], "chip", way.pairs(k)) for k in range(1, chips)
        ]

    start = warm_start[0]
    work = (2 * chips + 1,) + panel
    same0 = gather(start)
    keep, send = call(
        functools.partial(first_kernel, way),
        [stack, stack],
        [meta],
        [start, tiles],
        scratch=[work],
        flops=n * unit,
    )
    after, added = scatter(keep, send)
    gathered0 = forward(same0, after)
    base0, nbase0 = call(
        diag_kernel, [panel, panel], [], [start, diag, ndiag], flops=4 * unit
    )
    residual, keep, send = call(
        functools.partial(residual_kernel, way),
        [panel, stack, stack],
        [meta],
        [base0, target, gathered0, tiles, added],
        scratch=[work],
        flops=2 * n * unit,
    )
    same1 = gather(residual)
    after, added = scatter(keep, send)
    gathered1 = forward(same1, after)
    base1, nbase1, newton_start = call(
        functools.partial(diag_half_kernel, way),
        [panel] * 3,
        [meta],
        [residual, diag, ndiag, nbase0, gathered0, ntiles],
        flops=2 * (n + 2) * unit,
    )
    image, half_residual, sums = call(
        functools.partial(image_kernel, way),
        [panel, panel, (3, count)],
        [meta],
        [residual, base1, gathered1, tiles, added],
        flops=n * unit,
    )
    gathered2 = forward(gather(image))
    all_sums = lax.all_to_all(
        jnp.broadcast_to(sums[None], (devices,) + sums.shape), ALL, 0, 0, tiled=True
    )
    base2, nbase2, newton_residual = call(
        functools.partial(diag_half_kernel, way),
        [panel] * 3,
        [meta],
        [image, diag, ndiag, nbase1, gathered1, ntiles],
        flops=2 * (n + 2) * unit,
    )
    hr, hc = count // groups, count // columns
    depth = -(-(hc + 1) // 8) * 8
    share = (devices // 2, depth, LANES)
    x1, d1, norm, keep, send = call(
        functools.partial(middle_kernel, way, groups, columns),
        [panel, panel, (1, count), share, share],
        [meta],
        [
            gathered2,
            tiles,
            ntiles,
            base2,
            nbase2,
            all_sums,
            start,
            residual,
            half_residual,
            newton_start,
            newton_residual,
        ],
        scratch=[
            (2,) + share,
            (2, 2 * count, size),
            (2 * count, 2 * count),
            (count, LANES),
        ],
        flops=4 * n * unit,
    )
    received = lax.ppermute(send, "core", swap)
    received = lax.all_to_all(keep + received, ("row", "chip"), 0, 0, tiled=True)
    solved, hessian = call(
        functools.partial(last_kernel, groups, columns),
        [panel, (hc, count // groups)],
        [place],
        [received, norm, x1, d1],
        flops=unit // 100,
    )
    return solved[None], hessian.T


def solution(mesh):
    rows, columns = mesh.devices.shape
    fine = Mesh(mesh.devices.reshape(rows, columns // 2, 2), ALL)
    placed = (
        P(ALL, None, None),
        P(ALL, None, None, None),
        P(ALL, None),
        P(ALL, None, None),
        P(ALL, None, None, None),
        P(ALL, None, None),
        P(),
    )
    return jax.shard_map(
        on_device,
        mesh=fine,
        in_specs=placed,
        out_specs=(P(ALL, None, None), P("row", ("chip", "core"))),
        check_vma=False,
    )
```

```python
import functools

import jax
import jax.numpy as jnp
from jax import lax
from jax.experimental import pallas as pl
from jax.experimental.pallas import tpu as pltpu
from jax.sharding import Mesh, PartitionSpec as P


F32 = jnp.float32
BF16 = jnp.bfloat16
ALL = ("row", "chip", "core")
GRANT = 24 << 20
LANES = 128
HALF = 64

NT = (((1,), (1,)), ((), ()))
NN = (((1,), (0,)), ((), ()))


def split(value):
    high = value.astype(BF16)
    low = (value - high.astype(F32)).astype(BF16)
    return high, low


def dot3(left, right, dims):
    rows = left[0].shape[0]
    both = jnp.concatenate(left, axis=0)
    first = lax.dot_general(both, right[0], dims, preferred_element_type=F32)
    second = lax.dot_general(left[0], right[1], dims, preferred_element_type=F32)
    return first[:rows] + first[rows:] + second


def dot_full(left, right, dims):
    return lax.dot_general(
        left, right, dims, precision=lax.Precision.HIGHEST, preferred_element_type=F32
    )


def row_sums(product):
    return dot_full(jnp.ones((8, product.shape[1]), F32), product, NT)[0:1]


def column_of(row):
    n = row.shape[1]
    eye = lax.broadcasted_iota(jnp.int32, (n, n), 0) == lax.broadcasted_iota(
        jnp.int32, (n, n), 1
    )
    return jnp.sum(jnp.where(eye, row, 0.0), axis=1, keepdims=True)


class Far:
    def __init__(self, array, anywhere=False):
        self.stacked = isinstance(array, (tuple, list))
        self.arrays = list(array) if self.stacked else [array]
        if not anywhere:
            self.arrays = [
                pltpu.with_memory_space_constraint(a, pltpu.HBM) for a in self.arrays
            ]
        first = self.arrays[0]
        self.shape = (len(self.arrays),) * self.stacked + first.shape
        self.pieces = self.shape[0] if len(self.shape) == 3 else 1
        self.dtype = first.dtype

    def copies(self, refs, buffer, sems):
        for k in range(self.pieces):
            if self.stacked:
                source, target = refs[k], buffer.at[k]
            elif len(self.shape) == 3:
                source, target = refs[0].at[k], buffer.at[k]
            else:
                source, target = refs[0], buffer
            yield pltpu.make_async_copy(source, target, sems.at[k])


class Fetched:
    def __init__(self, copies, ref):
        self.copies, self.ref, self.shape = copies, ref, ref.shape

    def wait(self):
        for copy in self.copies:
            copy.wait()
        self.copies = []
        return self.ref

    def all(self):
        return self.wait()[...]


def call(body, outs, scalars, operands, scratch=(), flops=0):
    flat, plan = [], []
    for one in operands:
        arrays = one.arrays if isinstance(one, Far) else one
        if not isinstance(arrays, (tuple, list)):
            arrays = [arrays]
        plan.append((one, len(flat), len(arrays)))
        flat.extend(arrays)
    fars = [one for one, _, _ in plan if isinstance(one, Far)]
    smem = pl.BlockSpec(memory_space=pltpu.SMEM)
    vmem = pl.BlockSpec(memory_space=pltpu.VMEM)
    specs = [smem] * len(scalars)
    for one, _, length in plan:
        specs += [pl.BlockSpec(memory_space=pl.ANY) if isinstance(one, Far) else vmem] * length

    def kernel(*refs):
        given, refs = refs[: len(scalars)], refs[len(scalars) :]
        arrays, refs = refs[: len(flat)], refs[len(flat) :]
        out, refs = refs[: len(outs)], refs[len(outs) :]
        mine, refs = refs[: len(scratch)], refs[len(scratch) :]
        buffers, sems = refs[: len(fars)], refs[len(fars) :]
        seen, at = [], 0
        for one, first, length in plan:
            if isinstance(one, Far):
                copies = list(
                    one.copies(arrays[first : first + length], buffers[at], sems[at])
                )
                for copy in copies:
                    copy.start()
                seen.append(Fetched(copies, buffers[at]))
                at += 1
            elif isinstance(one, (tuple, list)):
                seen.append(arrays[first : first + length])
            else:
                seen.append(arrays[first])
        body(*given, *seen, *out, *mine)

    outs = [o if isinstance(o, jax.ShapeDtypeStruct) else jax.ShapeDtypeStruct(o, F32) for o in outs]
    scratch = [o if isinstance(o, jax.ShapeDtypeStruct) else jax.ShapeDtypeStruct(o, F32) for o in scratch]
    return pl.pallas_call(
        kernel,
        out_shape=outs,
        in_specs=specs,
        out_specs=[vmem] * len(outs),
        scratch_shapes=[pltpu.VMEM(o.shape, o.dtype) for o in scratch]
        + [pltpu.VMEM(one.shape, one.dtype) for one in fars]
        + [pltpu.SemaphoreType.DMA((one.pieces,)) for one in fars],
        cost_estimate=pl.CostEstimate(
            flops=flops,
            bytes_accessed=sum(a.size * a.dtype.itemsize for a in flat),
            transcendentals=0,
        ),
        compiler_params=pltpu.CompilerParams(vmem_limit_bytes=GRANT),
    )(*scalars, *flat)


class Way:
    def __init__(self, chips):
        self.chips, self.power = chips, chips & (chips - 1) == 0

    def pairs(self, k):
        n = self.chips
        return [(i, i ^ k if self.power else (i + k) % n) for i in range(n)]

    def to(self, here, there):
        n = self.chips
        return there ^ here if self.power else lax.rem(there - here + n, n)

    def source(self, k):
        return k if self.power else (self.chips - k) % self.chips


def seats(way, meta, count):
    chip, core = meta[count], meta[count + 1]
    found = []
    for k in range(count):
        slot = jnp.maximum(meta[k], 0)
        kind = jnp.where(slot % 2 == core, 0, way.chips)
        found.append(
            jnp.where(meta[k] >= 0, kind + way.to(chip, slot // 2), 2 * way.chips)
        )
    return found


def contributions(way, meta, pairs, panel, work, keep, send):
    chips = way.chips
    work[0 : 2 * chips] = jnp.zeros((2 * chips,) + work.shape[1:], F32)
    for seat, pair in zip(seats(way, meta, len(pairs)), pairs):
        work[seat] = dot3(panel, pair(), NN)
    keep[...] = work[0:chips]
    send[...] = work[chips : 2 * chips]


def hold(gathered, held):
    for k, block in enumerate(gathered):
        high, low = split(block[...])
        rows = high.shape[0]
        held[k, 0:rows] = high
        held[k, rows : 2 * rows] = low
    held[len(gathered)] = jnp.zeros(held.shape[1:], BF16)


def off_diagonal(way, meta, pairs, held):
    rows = held.shape[1] // 2
    first = second = None
    for seat, pair in zip(seats(way, meta, len(pairs)), pairs):
        both, (high, low) = held[seat], pair()
        one = lax.dot_general(both, high, NT, preferred_element_type=F32)
        two = lax.dot_general(both[:rows], low, NT, preferred_element_type=F32)
        first = one if first is None else first + one
        second = two if second is None else second + two
    return first[:rows] + (first[rows:] + second)


def held_pairs(split_tiles):
    return [
        functools.partial(lambda k: (split_tiles[0, k], split_tiles[1, k]), k)
        for k in range(split_tiles.shape[1])
    ]


def fresh_pairs(tiles):
    return [
        functools.partial(lambda k: split(tiles.ref[k]), k)
        for k in range(tiles.shape[0])
    ]


def first_kernel(way, meta, panel, tiles, keep, send, work):
    tiles.wait()
    contributions(way, meta, fresh_pairs(tiles), split(panel[...]), work, keep, send)


def prepare_kernel(panel, diag, tiles, image, split_tiles):
    image[...] = dot_full(panel[...], diag.all(), NT)
    tiles.wait()
    for k in range(tiles.shape[0]):
        split_tiles[0, k], split_tiles[1, k] = split(tiles.ref[k])


def residual_kernel(
    way, meta, base, target, gathered, split_tiles, added, residual, keep, send, work, held
):
    pairs = held_pairs(split_tiles)
    hold(gathered, held)
    total = base[...] + off_diagonal(way, meta, pairs, held)
    for block in added:
        total = total + block[...]
    rows, size = residual.shape
    unit = target[...] == lax.broadcasted_iota(jnp.int32, (rows, size), 1)
    value = unit.astype(F32) - total
    residual[...] = value
    contributions(way, meta, pairs, split(value), work, keep, send)


def image_kernel(way, meta, panel, base, gathered, split_tiles, added, image, sums, held):
    hold(gathered, held)
    total = base[...] + off_diagonal(way, meta, held_pairs(split_tiles), held)
    for block in added:
        total = total + block[...]
    image[...] = total
    value = panel[...]
    sums[0:1] = row_sums(value * value)
    sums[1:2] = row_sums(value * total)
    sums[2:3] = row_sums(total * total)


def middle_kernel(
    way,
    parts_rows,
    parts_cols,
    meta,
    sums,
    images,
    starts,
    residuals,
    split_tiles,
    diag,
    newton_diag,
    newton_tiles,
    x_out,
    d_out,
    norm_out,
    keep,
    send,
    held,
    packed,
    order,
    blocks,
    pieces,
):
    n = split_tiles.shape[1]
    totals = sums[0]
    for device in range(1, sums.shape[0]):
        totals = totals + sums[device]
    rr, rq, qq = totals[0:1], totals[1:2], totals[2:3]
    step = rr / rq
    norm = rr - 2.0 * step * rq + step * step * qq
    norm_out[...] = norm
    step_col = column_of(step)
    grow = 1.0 + column_of(norm / rr)
    count, _ = x_out.shape
    starts.wait()
    residuals.wait()
    for k, image in enumerate(images):
        r = residuals.ref[k]
        x = starts.ref[k] + step_col * r
        d = grow * r - step_col * image[...]
        if k == 0:
            x_out[...] = x
            d_out[...] = d
        held[k, 0:count], held[k, 3 * count : 4 * count] = split(x)
        held[k, count : 2 * count], held[k, 2 * count : 3 * count] = split(d)
    held[len(images)] = jnp.zeros(held.shape[1:], BF16)
    x1, d1 = x_out[...], d_out[...]
    found = seats(way, meta, n)

    def product(rows, tile):
        return lax.dot_general(rows, tile, NT, preferred_element_type=F32)

    high, low = split(diag.all() * 0.5)
    own = held[0]
    first = product(own[count : 3 * count], high)
    second = product(own[count : 2 * count], low)
    for k in range(n):
        block = held[found[k]]
        first += product(block[count : 3 * count], split_tiles[0, k])
        second += product(block[count : 2 * count], split_tiles[1, k])
    half_d = first[:count] + (first[count:] + second)
    curvature = 2.0 * row_sums(d1 * half_d)
    high, low = split(newton_diag.all() * 0.5)
    first = product(own, high)
    second = product(own[: 2 * count], low)
    newton_tiles.wait()
    for k in range(n):
        block = held[found[k]]
        high, low = split(newton_tiles.ref[k])
        first += product(block, high)
        second += product(block[: 2 * count], low)
    ux = first[:count] + (first[3 * count :] + second[:count])
    ud = first[count : 2 * count] + (first[2 * count : 3 * count] + second[count:])
    hr, hc = count // parts_rows, count // parts_cols
    for r_index in range(parts_rows):
        for kind, pair in enumerate(((x1, ux), (d1, ud))):
            at = (2 * r_index + kind) * hr
            for side in range(2):
                order[side, at : at + hr] = pair[side][
                    r_index * hr : (r_index + 1) * hr
                ]
    blocks[...] = dot_full(
        jnp.concatenate([x1, d1], axis=0), order[1], NT
    ) + dot_full(jnp.concatenate([ux, ud], axis=0), order[0], NT)
    core = meta[n + 1]
    for r_index in range(parts_rows):
        lanes = slice(2 * r_index * hr, 2 * (r_index + 1) * hr)
        pieces[:, 0 : 2 * hr] = blocks[0:count, lanes]
        pieces[:, HALF : HALF + 2 * hr] = blocks[count : 2 * count, lanes]
        for c_index in range(parts_cols):
            at = r_index * (parts_cols // 2) + c_index // 2
            target = packed.at[c_index % 2, at]
            target[0:hc] = pieces[c_index * hc : (c_index + 1) * hc]
            target[hc : hc + 1, 0:count] = curvature
    keep[...] = packed[core]
    send[...] = packed[1 - core]


def last_kernel(parts_rows, parts_cols, n, meta, received, norm, x1, d1, x_out, hessian):
    total = received[0]
    for device in range(1, received.shape[0]):
        total = total + received[device]
    count = x1.shape[0]
    hr, hc = count // parts_rows, count // parts_cols
    step = norm[...] / total[hc : hc + 1, 0:count]
    step_col = column_of(step)
    x_out[...] = x1[...] + step_col * d1[...]
    row_at, col_at = meta[n + 2] * hr, (meta[n] * 2 + meta[n + 1]) * hc
    wanted = lax.broadcasted_iota(jnp.int32, (count, hr), 0) == row_at + (
        lax.broadcasted_iota(jnp.int32, (count, hr), 1)
    )
    of_rows = jnp.sum(jnp.where(wanted, step_col, 0.0), axis=0, keepdims=True)
    wanted = lax.broadcasted_iota(jnp.int32, (hc, count), 1) == col_at + (
        lax.broadcasted_iota(jnp.int32, (hc, count), 0)
    )
    of_cols = jnp.sum(jnp.where(wanted, step, 0.0), axis=1, keepdims=True)
    xx = total[0:hc, 0:hr]
    dx = total[0:hc, hr : 2 * hr]
    xd = total[0:hc, HALF : HALF + hr]
    dd = total[0:hc, HALF + hr : HALF + 2 * hr]
    hessian[...] = xx + of_rows * dx + of_cols * (xd + of_rows * dd)


def on_device(
    precision_diag,
    precision_pairs,
    pattern_cols,
    newton_diag,
    newton_pairs,
    warm_start,
    target_rows,
):
    groups = lax.axis_size("row")
    chips = lax.axis_size("chip")
    columns = chips * 2
    devices = groups * columns
    row, chip, core = (lax.axis_index(a).astype(jnp.int32) for a in ALL)
    block = row * columns + chip * 2 + core
    count, size = warm_start.shape[1:]
    n = precision_pairs.shape[1]
    spot = jnp.arange(n + 3, dtype=jnp.int32)
    slots = jnp.where(pattern_cols >= 0, pattern_cols - row * columns, -1)[0]
    meta = jnp.where(spot == n, chip, jnp.where(spot == n + 1, core, row))
    meta = jnp.where(spot < n, jnp.pad(slots, (0, 3)), meta)
    target = (target_rows - block * size).astype(jnp.int32)[:, None]
    tiles, diag = precision_pairs[0], precision_diag[0]
    ntiles, ndiag = newton_pairs[0], newton_diag[0]
    panel = (count, size)
    stack = (chips, count, size)
    swap = [(0, 1), (1, 0)]
    way = Way(chips)
    unit = 2 * count * size * size * 3
    parts = jax.ShapeDtypeStruct((2, n, size, size), BF16)
    work = (2 * chips + 1,) + panel
    held = jax.ShapeDtypeStruct((2 * chips + 1, 2 * count, size), BF16)

    def gather(value):
        same = [value] + [None] * (chips - 1)
        for k in range(1, chips):
            same[way.source(k)] = lax.ppermute(value, "chip", way.pairs(k))
        return same

    def forward(same):
        return list(same) + [lax.ppermute(block, "core", swap) for block in same]

    def scatter(keep, send):
        received = lax.ppermute(send, "core", swap)
        sums = [keep[k] + received[k] for k in range(chips)]
        return [sums[0]] + [lax.ppermute(sums[k], "chip", way.pairs(k)) for k in range(1, chips)]

    def prepare(value):
        return call(
            prepare_kernel,
            [panel, parts],
            [],
            [value, Far(diag), Far(tiles)],
            flops=4 * unit,
        )

    start = warm_start[0]
    starts = gather(start)
    keep, send = call(
        functools.partial(first_kernel, way),
        [stack, stack],
        [meta],
        [start, Far(tiles)],
        scratch=[work],
        flops=n * unit,
    )
    added = scatter(keep, send)
    starts = forward(starts)
    base, split_tiles = prepare(start)
    residual, keep, send = call(
        functools.partial(residual_kernel, way),
        [panel, stack, stack],
        [meta],
        [base, target, starts, split_tiles, added],
        scratch=[work, held],
        flops=2 * n * unit,
    )
    residuals = gather(residual)
    added = scatter(keep, send)
    residuals = forward(residuals)
    base, split_tiles = prepare(residual)
    image, sums = call(
        functools.partial(image_kernel, way),
        [panel, (3, count)],
        [meta],
        [residual, base, residuals, split_tiles, added],
        scratch=[held],
        flops=n * unit,
    )
    images = gather(image)
    all_sums = lax.all_to_all(
        jnp.broadcast_to(sums[None], (devices,) + sums.shape), ALL, 0, 0, tiled=True
    )
    images = forward(images)
    _, split_tiles = prepare(image)
    hr, hc = count // groups, count // columns
    depth = -(-(hc + 1) // 8) * 8
    share = (devices // 2, depth, LANES)
    x1, d1, norm, keep, send = call(
        functools.partial(middle_kernel, way, groups, columns),
        [panel, panel, (1, count), share, share],
        [meta],
        [
            all_sums,
            images,
            Far(starts, anywhere=True),
            Far(residuals, anywhere=True),
            split_tiles,
            Far(diag),
            Far(ndiag),
            Far(ntiles),
        ],
        scratch=[
            jax.ShapeDtypeStruct((2 * chips + 1, 4 * count, size), BF16),
            (2,) + share,
            (2, 2 * count, size),
            (2 * count, 2 * count),
            (count, LANES),
        ],
        flops=4 * n * unit,
    )
    received = lax.ppermute(send, "core", swap)
    received = lax.all_to_all(keep + received, ("row", "chip"), 0, 0, tiled=True)
    solved, hessian = call(
        functools.partial(last_kernel, groups, columns, n),
        [panel, (hc, hr)],
        [meta],
        [received, norm, x1, d1],
        flops=unit // 100,
    )
    return solved[None], hessian.T


def solution(mesh):
    rows, columns = mesh.devices.shape
    fine = Mesh(mesh.devices.reshape(rows, columns // 2, 2), ALL)
    placed = (
        P(ALL, None, None),
        P(ALL, None, None, None),
        P(ALL, None),
        P(ALL, None, None),
        P(ALL, None, None, None),
        P(ALL, None, None),
        P(),
    )
    return jax.shard_map(
        on_device,
        mesh=fine,
        in_specs=placed,
        out_specs=(P(ALL, None, None), P("row", ("chip", "core"))),
        check_vma=False,
    )
```

```python
import functools

import jax
import jax.numpy as jnp
from jax import lax
from jax.experimental import pallas as pl
from jax.experimental.pallas import tpu as pltpu
from jax.sharding import Mesh, PartitionSpec as P


F32 = jnp.float32
BF16 = jnp.bfloat16
ALL = ("row", "chip", "core")
GRANT = 24 << 20
LANES = 128
HALF = 64

NT = (((1,), (1,)), ((), ()))
NN = (((1,), (0,)), ((), ()))


def split(value):
    high = value.astype(BF16)
    low = (value - high.astype(F32)).astype(BF16)
    return high, low


def dot3(left, right, dims):
    rows = left[0].shape[0]
    both = jnp.concatenate(left, axis=0)
    first = lax.dot_general(both, right[0], dims, preferred_element_type=F32)
    second = lax.dot_general(left[0], right[1], dims, preferred_element_type=F32)
    return first[:rows] + first[rows:] + second


def dot_full(left, right, dims):
    return lax.dot_general(
        left, right, dims, precision=lax.Precision.HIGHEST, preferred_element_type=F32
    )


def row_sums(product):
    return dot_full(jnp.ones((8, product.shape[1]), F32), product, NT)[0:1]


def column_of(row):
    n = row.shape[1]
    eye = lax.broadcasted_iota(jnp.int32, (n, n), 0) == lax.broadcasted_iota(
        jnp.int32, (n, n), 1
    )
    return jnp.sum(jnp.where(eye, row, 0.0), axis=1, keepdims=True)


class Far:
    def __init__(self, array, space=pltpu.VMEM):
        self.arrays = [pltpu.with_memory_space_constraint(array, pltpu.HBM)]
        self.pieces = array.shape[0] if array.ndim == 3 else 1
        self.buffer = space(array.shape, array.dtype)

    def copies(self, ref, buffer, sems):
        if self.pieces == 1:
            return [pltpu.make_async_copy(ref, buffer, sems.at[0])]
        return [
            pltpu.make_async_copy(ref.at[k], buffer.at[k], sems.at[k])
            for k in range(self.pieces)
        ]


class Fetched:
    def __init__(self, copies, ref):
        self.copies, self.ref, self.shape, self.done = copies, ref, ref.shape, 0

    def wait(self, upto=None):
        upto = len(self.copies) if upto is None else upto
        for k in range(self.done, upto):
            self.copies[k].wait()
        self.done = max(self.done, upto)
        return self.ref

    def all(self):
        return self.wait()[...]


def call(body, outs, scalars, operands, scratch=(), flops=0):
    flat, plan = [], []
    for one in operands:
        arrays = one.arrays if isinstance(one, Far) else one
        if not isinstance(arrays, (tuple, list)):
            arrays = [arrays]
        plan.append((one, len(flat), len(arrays)))
        flat.extend(arrays)
    fars = [one for one, _, _ in plan if isinstance(one, Far)]
    smem = pl.BlockSpec(memory_space=pltpu.SMEM)
    vmem = pl.BlockSpec(memory_space=pltpu.VMEM)
    specs = [smem] * len(scalars)
    for one, _, length in plan:
        specs += [pl.BlockSpec(memory_space=pl.ANY) if isinstance(one, Far) else vmem] * length

    def kernel(*refs):
        given, refs = refs[: len(scalars)], refs[len(scalars) :]
        arrays, refs = refs[: len(flat)], refs[len(flat) :]
        out, refs = refs[: len(outs)], refs[len(outs) :]
        mine, refs = refs[: len(scratch)], refs[len(scratch) :]
        buffers, sems = refs[: len(fars)], refs[len(fars) :]
        seen, at = [], 0
        for one, first, length in plan:
            if isinstance(one, Far):
                copies = one.copies(arrays[first], buffers[at], sems[at])
                for copy in copies:
                    copy.start()
                seen.append(Fetched(copies, buffers[at]))
                at += 1
            elif isinstance(one, (tuple, list)):
                seen.append(arrays[first : first + length])
            else:
                seen.append(arrays[first])
        body(*given, *seen, *out, *mine)

    outs = [o if isinstance(o, jax.ShapeDtypeStruct) else jax.ShapeDtypeStruct(o, F32) for o in outs]
    scratch = [o if isinstance(o, jax.ShapeDtypeStruct) else jax.ShapeDtypeStruct(o, F32) for o in scratch]
    return pl.pallas_call(
        kernel,
        out_shape=outs,
        in_specs=specs,
        out_specs=[vmem] * len(outs),
        scratch_shapes=[pltpu.VMEM(o.shape, o.dtype) for o in scratch]
        + [one.buffer for one in fars]
        + [pltpu.SemaphoreType.DMA((one.pieces,)) for one in fars],
        cost_estimate=pl.CostEstimate(
            flops=flops,
            bytes_accessed=sum(a.size * a.dtype.itemsize for a in flat),
            transcendentals=0,
        ),
        compiler_params=pltpu.CompilerParams(vmem_limit_bytes=GRANT),
    )(*scalars, *flat)


class Way:
    def __init__(self, chips):
        self.chips, self.power = chips, chips & (chips - 1) == 0

    def pairs(self, k):
        n = self.chips
        return [(i, i ^ k if self.power else (i + k) % n) for i in range(n)]

    def to(self, here, there):
        n = self.chips
        return there ^ here if self.power else lax.rem(there - here + n, n)

    def source(self, k):
        return k if self.power else (self.chips - k) % self.chips


def seats(way, cols):
    chip, core = lax.axis_index("chip"), lax.axis_index("core")
    first = lax.axis_index("row") * (2 * way.chips)
    found = []
    for k in range(cols.shape[0]):
        slot = jnp.maximum(cols[k] - first, 0)
        kind = jnp.where(lax.rem(slot, 2) == core, 0, way.chips)
        found.append(
            jnp.where(cols[k] >= 0, kind + way.to(chip, slot // 2), 2 * way.chips)
        )
    return found


def contributions(way, cols, pairs, panel, work, keep, send):
    chips = way.chips
    work[0 : 2 * chips] = jnp.zeros((2 * chips,) + work.shape[1:], F32)
    for seat, pair in zip(seats(way, cols), pairs):
        work[seat] = dot3(panel, pair(), NN)
    keep[...] = work[0:chips]
    send[...] = work[chips : 2 * chips]


def hold(gathered, held):
    for k, block in enumerate(gathered):
        high, low = split(block[...])
        rows = high.shape[0]
        held[k, 0:rows] = high
        held[k, rows : 2 * rows] = low
    held[len(gathered)] = jnp.zeros(held.shape[1:], BF16)


def off_diagonal(way, cols, pairs, held):
    rows = held.shape[1] // 2
    first = second = None
    for seat, pair in zip(seats(way, cols), pairs):
        both, (high, low) = held[seat], pair()
        one = lax.dot_general(both, high, NT, preferred_element_type=F32)
        two = lax.dot_general(both[:rows], low, NT, preferred_element_type=F32)
        first = one if first is None else first + one
        second = two if second is None else second + two
    return first[:rows] + (first[rows:] + second)


def held_pairs(split_tiles):
    return [
        functools.partial(lambda k: (split_tiles[0, k], split_tiles[1, k]), k)
        for k in range(split_tiles.shape[1])
    ]


def fresh_pairs(tiles):
    n = tiles.shape[0]
    half = (n + 1) // 2

    def pair(k):
        if k in (0, half):
            tiles.wait(half if k == 0 else n)
        return split(tiles.ref[k])

    return [functools.partial(pair, k) for k in range(n)]


def first_kernel(way, cols, panel, tiles, keep, send, work):
    cols = cols.wait()
    contributions(way, cols, fresh_pairs(tiles), split(panel.all()), work, keep, send)


def prepare_kernel(panel, diag, tiles, image, split_tiles):
    image[...] = dot_full(panel.all(), diag.all(), NT)
    tiles.wait()
    for k in range(tiles.shape[0]):
        split_tiles[0, k], split_tiles[1, k] = split(tiles.ref[k])


def diag_kernel(panel, diag, image):
    image[...] = dot_full(panel[...], diag.all(), NT)


def residual_kernel(
    way, cols, base, target, gathered, split_tiles, added, residual, keep, send, work, held
):
    pairs = held_pairs(split_tiles)
    hold(gathered, held)
    total = base[...] + off_diagonal(way, cols, pairs, held)
    for block in added:
        total = total + block[...]
    rows, size = residual.shape
    chips = way.chips
    block = (lax.axis_index("row") * chips + lax.axis_index("chip")) * 2
    block = block + lax.axis_index("core")
    at = column_of((target[...] - block * size).astype(F32))
    unit = at == lax.broadcasted_iota(jnp.int32, (rows, size), 1).astype(F32)
    value = unit.astype(F32) - total
    residual[...] = value
    contributions(way, cols, pairs, split(value), work, keep, send)


def image_kernel(way, cols, panel, base, gathered, split_tiles, added, image, sums, held):
    hold(gathered, held)
    total = base[...] + off_diagonal(way, cols, held_pairs(split_tiles), held)
    for block in added:
        total = total + block[...]
    image[...] = total
    value = panel[...]
    found = jnp.concatenate(
        [row_sums(value * value), row_sums(value * total), row_sums(total * total)], 0
    )
    sums[...] = jnp.broadcast_to(found[None], sums.shape)


def steps(sums):
    totals = sums[0]
    for device in range(1, sums.shape[0]):
        totals = totals + sums[device]
    rr, rq, qq = totals[0:1], totals[1:2], totals[2:3]
    step = rr / rq
    norm = rr - 2.0 * step * rq + step * step * qq
    return norm, column_of(step), 1.0 + column_of(norm / rr)


def middle_kernel(
    way,
    parts_rows,
    parts_cols,
    cols,
    sums,
    starts,
    residuals,
    images,
    split_tiles,
    diag,
    newton_diag,
    newton_tiles,
    x_out,
    d_out,
    norm_out,
    keep,
    send,
    held,
    order,
    blocks,
    pieces,
):
    n = newton_tiles.shape[0]
    norm_out[...], step, grow = steps(sums)
    count = d_out.shape[0]
    for k, image in enumerate(images):
        r = residuals[k][...]
        x = starts[k][...] + step * r
        d = grow * r - step * image[...]
        if k == 0:
            x_out[...] = x
            d_out[...] = d
        held[k, 0:count], held[k, 3 * count : 4 * count] = split(x)
        held[k, count : 2 * count], held[k, 2 * count : 3 * count] = split(d)
    held[len(images)] = jnp.zeros(held.shape[1:], BF16)
    x1, d1 = x_out[...], d_out[...]
    found = seats(way, cols)

    def product(rows, tile):
        return lax.dot_general(rows, tile, NT, preferred_element_type=F32)

    high, low = split(diag.all() * 0.5)
    own = held[0]
    first = product(own[count : 3 * count], high)
    second = product(own[count : 2 * count], low)
    for k in range(n):
        block = held[found[k]]
        first += product(block[count : 3 * count], split_tiles[0, k])
        second += product(block[count : 2 * count], split_tiles[1, k])
    half_d = first[:count] + (first[count:] + second)
    curvature = 2.0 * row_sums(d1 * half_d)
    high, low = split(newton_diag.all() * 0.5)
    first = product(own, high)
    second = product(own[: 2 * count], low)
    for seat, pair in zip(found, fresh_pairs(newton_tiles)):
        block, (high, low) = held[seat], pair()
        first += product(block, high)
        second += product(block[: 2 * count], low)
    ux = first[:count] + (first[3 * count :] + second[:count])
    ud = first[count : 2 * count] + (first[2 * count : 3 * count] + second[count:])
    hr, hc = count // parts_rows, count // parts_cols
    for r_index in range(parts_rows):
        for kind, pair in enumerate(((x1, ux), (d1, ud))):
            at = r_index * HALF + kind * hr
            for side in range(2):
                order[side, at : at + hr] = pair[side][
                    r_index * hr : (r_index + 1) * hr
                ]
        at = r_index * HALF + 2 * hr
        order[:, at : (r_index + 1) * HALF] = jnp.zeros(
            (2, HALF - 2 * hr, x1.shape[1]), F32
        )
    blocks[...] = dot_full(
        jnp.concatenate([x1, d1], axis=0), order[1], NT
    ) + dot_full(jnp.concatenate([ux, ud], axis=0), order[0], NT)
    depth = keep.shape[1]
    left = lax.broadcasted_iota(jnp.int32, (count, LANES), 1) < HALF
    wide = jnp.concatenate([curvature, jnp.zeros((1, LANES - count), F32)], axis=1)
    spot = lax.broadcasted_iota(jnp.int32, (depth, LANES), 0) == hc
    first_core = lax.axis_index("core") == 0
    for r_index in range(parts_rows):
        lanes = slice(r_index // 2 * LANES, (r_index // 2 + 1) * LANES)
        top, bottom = blocks[0:count, lanes], blocks[count : 2 * count, lanes]
        if r_index % 2:
            top = pltpu.roll(top, HALF, 1)
        else:
            bottom = pltpu.roll(bottom, HALF, 1)
        pieces[r_index, 0:count] = jnp.where(left, top, bottom)
        for pair in range(parts_cols // 2):
            one, two = (
                jnp.where(spot, wide, pieces[r_index, c * hc : c * hc + depth])
                for c in (2 * pair, 2 * pair + 1)
            )
            at = r_index * (parts_cols // 2) + pair
            keep[at] = jnp.where(first_core, one, two)
            send[at] = jnp.where(first_core, two, one)


def last_kernel(parts_rows, parts_cols, received, norm, x1, d1, x_out, hessian):
    total = received[0]
    for device in range(1, received.shape[0]):
        total = total + received[device]
    count = x1.shape[0]
    hr, hc = count // parts_rows, count // parts_cols
    step = norm[...] / total[hc : hc + 1, 0:count]
    step_col = column_of(step)
    x_out[...] = x1[...] + step_col * d1[...]
    row_at = lax.axis_index("row") * hr
    col_at = (lax.axis_index("chip") * 2 + lax.axis_index("core")) * hc
    wanted = lax.broadcasted_iota(jnp.int32, (count, hr), 0) == row_at + (
        lax.broadcasted_iota(jnp.int32, (count, hr), 1)
    )
    of_rows = jnp.sum(jnp.where(wanted, step_col, 0.0), axis=0, keepdims=True)
    wanted = lax.broadcasted_iota(jnp.int32, (hc, count), 1) == col_at + (
        lax.broadcasted_iota(jnp.int32, (hc, count), 0)
    )
    of_cols = jnp.sum(jnp.where(wanted, step, 0.0), axis=1, keepdims=True)
    xx = total[0:hc, 0:hr]
    dx = total[0:hc, hr : 2 * hr]
    xd = total[0:hc, HALF : HALF + hr]
    dd = total[0:hc, HALF + hr : HALF + 2 * hr]
    hessian[...] = xx + of_rows * dx + of_cols * (xd + of_rows * dd)


def on_device(
    precision_diag,
    precision_pairs,
    pattern_cols,
    newton_diag,
    newton_pairs,
    warm_start,
    target_rows,
):
    groups = lax.axis_size("row")
    chips = lax.axis_size("chip")
    columns = chips * 2
    count, size = warm_start.shape[1:]
    n = precision_pairs.shape[1]
    cols = pattern_cols[0]
    target = target_rows[None]
    tiles, diag = precision_pairs[0], precision_diag[0]
    ntiles, ndiag = newton_pairs[0], newton_diag[0]
    panel = (count, size)
    stack = (chips, count, size)
    swap = [(0, 1), (1, 0)]
    way = Way(chips)
    unit = 2 * count * size * size * 3
    parts = jax.ShapeDtypeStruct((2, n, size, size), BF16)
    work = (2 * chips + 1,) + panel
    held = jax.ShapeDtypeStruct((2 * chips + 1, 2 * count, size), BF16)

    def gather(value):
        same = [value] + [None] * (chips - 1)
        for k in range(1, chips):
            same[way.source(k)] = lax.ppermute(value, "chip", way.pairs(k))
        return same

    def forward(same):
        return list(same) + [lax.ppermute(block, "core", swap) for block in same]

    def scatter(keep, send):
        received = lax.ppermute(send, "core", swap)
        sums = [keep[k] + received[k] for k in range(chips)]
        return [sums[0]] + [lax.ppermute(sums[k], "chip", way.pairs(k)) for k in range(1, chips)]

    start = warm_start[0]
    starts = gather(start)
    keep, send = call(
        functools.partial(first_kernel, way),
        [stack, stack],
        [],
        [Far(cols, pltpu.SMEM), Far(start), Far(tiles)],
        scratch=[work],
        flops=n * unit,
    )
    added = scatter(keep, send)
    starts = forward(starts)
    base, split_tiles = call(
        prepare_kernel,
        [panel, parts],
        [],
        [Far(start), Far(diag), Far(tiles)],
        flops=4 * unit,
    )
    residual, keep, send = call(
        functools.partial(residual_kernel, way),
        [panel, stack, stack],
        [cols],
        [base, target, starts, split_tiles, added],
        scratch=[work, held],
        flops=2 * n * unit,
    )
    residuals = gather(residual)
    added = scatter(keep, send)
    residuals = forward(residuals)
    (base,) = call(
        diag_kernel, [panel], [], [residual, Far(diag)], flops=2 * unit
    )
    image, sums = call(
        functools.partial(image_kernel, way),
        [panel, (groups * columns, 3, count)],
        [cols],
        [residual, base, residuals, split_tiles, added],
        scratch=[held],
        flops=n * unit,
    )
    images = gather(image)
    sums = lax.all_to_all(sums, ALL, 0, 0, tiled=True)
    images = forward(images)
    hr, hc = count // groups, count // columns
    depth = -(-(hc + 1) // 8) * 8
    share = (groups * chips, depth, LANES)
    x1, d1, norm, keep, send = call(
        functools.partial(middle_kernel, way, groups, columns),
        [panel, panel, (1, count), share, share],
        [cols],
        [
            sums,
            starts,
            residuals,
            images,
            split_tiles,
            Far(diag),
            Far(ndiag),
            Far(ntiles),
        ],
        scratch=[
            jax.ShapeDtypeStruct((2 * chips + 1, 4 * count, size), BF16),
            (2, groups * HALF, size),
            (2 * count, groups * HALF),
            (groups, count + depth, LANES),
        ],
        flops=4 * n * unit,
    )
    received = lax.ppermute(send, "core", swap)
    received = lax.all_to_all(keep + received, ("row", "chip"), 0, 0, tiled=True)
    solved, hessian = call(
        functools.partial(last_kernel, groups, columns),
        [panel, (hc, hr)],
        [],
        [received, norm, x1, d1],
        flops=unit // 100,
    )
    return solved[None], hessian.T


def solution(mesh):
    rows, columns = mesh.devices.shape
    fine = Mesh(mesh.devices.reshape(rows, columns // 2, 2), ALL)
    placed = (
        P(ALL, None, None),
        P(ALL, None, None, None),
        P(ALL, None),
        P(ALL, None, None),
        P(ALL, None, None, None),
        P(ALL, None, None),
        P(),
    )
    return jax.shard_map(
        on_device,
        mesh=fine,
        in_specs=placed,
        out_specs=(P(ALL, None, None), P("row", ("chip", "core"))),
        check_vma=False,
    )
```

```python
import functools

import jax
import jax.numpy as jnp
from jax import lax
from jax.experimental import pallas as pl
from jax.experimental.pallas import tpu as pltpu
from jax.sharding import Mesh, PartitionSpec as P


F32 = jnp.float32
BF16 = jnp.bfloat16
ALL = ("row", "chip", "core")
GRANT = 24 << 20
LANES = 128
HALF = 64

NT = (((1,), (1,)), ((), ()))
NN = (((1,), (0,)), ((), ()))


def split(value):
    high = value.astype(BF16)
    low = (value - high.astype(F32)).astype(BF16)
    return high, low


def dot3(left, right, dims):
    rows = left[0].shape[0]
    both = jnp.concatenate(left, axis=0)
    first = lax.dot_general(both, right[0], dims, preferred_element_type=F32)
    second = lax.dot_general(left[0], right[1], dims, preferred_element_type=F32)
    return first[:rows] + first[rows:] + second


def dot_full(left, right, dims):
    return lax.dot_general(
        left, right, dims, precision=lax.Precision.HIGHEST, preferred_element_type=F32
    )


def row_sums(product):
    return dot_full(jnp.ones((8, product.shape[1]), F32), product, NT)[0:1]


def column_of(row):
    n = row.shape[1]
    eye = lax.broadcasted_iota(jnp.int32, (n, n), 0) == lax.broadcasted_iota(
        jnp.int32, (n, n), 1
    )
    return jnp.sum(jnp.where(eye, row, 0.0), axis=1, keepdims=True)


class Far:
    def __init__(self, array, space=pltpu.VMEM):
        self.arrays = [pltpu.with_memory_space_constraint(array, pltpu.HBM)]
        self.pieces = array.shape[0] if array.ndim == 3 else 1
        self.buffer = space(array.shape, array.dtype)

    def copies(self, ref, buffer, sems):
        if self.pieces == 1:
            return [pltpu.make_async_copy(ref, buffer, sems.at[0])]
        return [
            pltpu.make_async_copy(ref.at[k], buffer.at[k], sems.at[k])
            for k in range(self.pieces)
        ]


class Fetched:
    def __init__(self, copies, ref):
        self.copies, self.ref, self.shape, self.done = copies, ref, ref.shape, 0

    def wait(self, upto=None):
        upto = len(self.copies) if upto is None else upto
        for k in range(self.done, upto):
            self.copies[k].wait()
        self.done = max(self.done, upto)
        return self.ref

    def all(self):
        return self.wait()[...]


def call(body, outs, scalars, operands, scratch=(), flops=0):
    flat, plan = [], []
    for one in operands:
        arrays = one.arrays if isinstance(one, Far) else one
        if not isinstance(arrays, (tuple, list)):
            arrays = [arrays]
        plan.append((one, len(flat), len(arrays)))
        flat.extend(arrays)
    fars = [one for one, _, _ in plan if isinstance(one, Far)]
    smem = pl.BlockSpec(memory_space=pltpu.SMEM)
    vmem = pl.BlockSpec(memory_space=pltpu.VMEM)
    specs = [smem] * len(scalars)
    for one, _, length in plan:
        specs += [pl.BlockSpec(memory_space=pl.ANY) if isinstance(one, Far) else vmem] * length

    def kernel(*refs):
        given, refs = refs[: len(scalars)], refs[len(scalars) :]
        arrays, refs = refs[: len(flat)], refs[len(flat) :]
        out, refs = refs[: len(outs)], refs[len(outs) :]
        mine, refs = refs[: len(scratch)], refs[len(scratch) :]
        buffers, sems = refs[: len(fars)], refs[len(fars) :]
        seen, at = [], 0
        for one, first, length in plan:
            if isinstance(one, Far):
                copies = one.copies(arrays[first], buffers[at], sems[at])
                for copy in copies:
                    copy.start()
                seen.append(Fetched(copies, buffers[at]))
                at += 1
            elif isinstance(one, (tuple, list)):
                seen.append(arrays[first : first + length])
            else:
                seen.append(arrays[first])
        body(*given, *seen, *out, *mine)

    outs = [o if isinstance(o, jax.ShapeDtypeStruct) else jax.ShapeDtypeStruct(o, F32) for o in outs]
    scratch = [o if isinstance(o, jax.ShapeDtypeStruct) else jax.ShapeDtypeStruct(o, F32) for o in scratch]
    return pl.pallas_call(
        kernel,
        out_shape=outs,
        in_specs=specs,
        out_specs=[vmem] * len(outs),
        scratch_shapes=[pltpu.VMEM(o.shape, o.dtype) for o in scratch]
        + [one.buffer for one in fars]
        + [pltpu.SemaphoreType.DMA((one.pieces,)) for one in fars],
        cost_estimate=pl.CostEstimate(
            flops=flops,
            bytes_accessed=sum(a.size * a.dtype.itemsize for a in flat),
            transcendentals=0,
        ),
        compiler_params=pltpu.CompilerParams(vmem_limit_bytes=GRANT),
    )(*scalars, *flat)


class Way:
    def __init__(self, chips):
        self.chips, self.power = chips, chips & (chips - 1) == 0

    def pairs(self, k):
        n = self.chips
        return [(i, i ^ k if self.power else (i + k) % n) for i in range(n)]

    def to(self, here, there):
        n = self.chips
        return there ^ here if self.power else lax.rem(there - here + n, n)

    def source(self, k):
        return k if self.power else (self.chips - k) % self.chips


def seats(way, cols):
    chip, core = lax.axis_index("chip"), lax.axis_index("core")
    first = lax.axis_index("row") * (2 * way.chips)
    found = []
    for k in range(cols.shape[0]):
        slot = jnp.maximum(cols[k] - first, 0)
        kind = jnp.where(lax.rem(slot, 2) == core, 0, way.chips)
        found.append(
            jnp.where(cols[k] >= 0, kind + way.to(chip, slot // 2), 2 * way.chips)
        )
    return found


def contributions(way, cols, pairs, panel, work, keep, send):
    chips = way.chips
    work[0 : 2 * chips] = jnp.zeros((2 * chips,) + work.shape[1:], F32)
    for seat, pair in zip(seats(way, cols), pairs):
        work[seat] = dot3(panel, pair(), NN)
    keep[...] = work[0:chips]
    send[...] = work[chips : 2 * chips]


def hold(gathered, held):
    for k, block in enumerate(gathered):
        high, low = split(block[...])
        rows = high.shape[0]
        held[k, 0:rows] = high
        held[k, rows : 2 * rows] = low
    held[len(gathered)] = jnp.zeros(held.shape[1:], BF16)


def off_diagonal(way, cols, pairs, held):
    rows = held.shape[1] // 2
    first = second = None
    for seat, pair in zip(seats(way, cols), pairs):
        both, (high, low) = held[seat], pair()
        one = lax.dot_general(both, high, NT, preferred_element_type=F32)
        two = lax.dot_general(both[:rows], low, NT, preferred_element_type=F32)
        first = one if first is None else first + one
        second = two if second is None else second + two
    return first[:rows] + (first[rows:] + second)


def held_pairs(split_tiles):
    return [
        functools.partial(lambda k: (split_tiles[0, k], split_tiles[1, k]), k)
        for k in range(split_tiles.shape[1])
    ]


def first_kernel(way, cols, panel, tiles, keep, send, split_tiles, work):
    cols = cols.wait()
    n = split_tiles.shape[1]

    def pair(k):
        if k in (0, (n + 1) // 2):
            tiles.wait(n if k else (n + 1) // 2)
        high, low = split(tiles.ref[k])
        split_tiles[0, k], split_tiles[1, k] = high, low
        return high, low

    pairs = [functools.partial(pair, k) for k in range(n)]
    contributions(way, cols, pairs, split(panel.all()), work, keep, send)


def diag_kernel(panel, diag, image):
    image[...] = dot_full(panel[...], diag[...], NT)


def diag_split_kernel(panel, diag, tiles, image, split_tiles):
    diag_kernel(panel, diag, image)
    for k in range(tiles.shape[0]):
        split_tiles[0, k], split_tiles[1, k] = split(tiles[k])


def residual_kernel(
    way, cols, base, target, gathered, split_tiles, added, residual, keep, send, work, held
):
    pairs = held_pairs(split_tiles)
    hold(gathered, held)
    total = base[...] + off_diagonal(way, cols, pairs, held)
    for block in added:
        total = total + block[...]
    rows, size = residual.shape
    chips = way.chips
    block = (lax.axis_index("row") * chips + lax.axis_index("chip")) * 2
    block = block + lax.axis_index("core")
    at = column_of((target[...] - block * size).astype(F32))
    unit = at == lax.broadcasted_iota(jnp.int32, (rows, size), 1).astype(F32)
    value = unit.astype(F32) - total
    residual[...] = value
    contributions(way, cols, pairs, split(value), work, keep, send)


def image_kernel(way, cols, panel, base, gathered, split_tiles, added, image, sums, held):
    hold(gathered, held)
    total = base[...] + off_diagonal(way, cols, held_pairs(split_tiles), held)
    for block in added:
        total = total + block[...]
    image[...] = total
    value = panel[...]
    found = jnp.concatenate(
        [row_sums(value * value), row_sums(value * total), row_sums(total * total)], 0
    )
    sums[...] = jnp.broadcast_to(found[None], sums.shape)


def steps(sums):
    totals = sums[0]
    for device in range(1, sums.shape[0]):
        totals = totals + sums[device]
    rr, rq, qq = totals[0:1], totals[1:2], totals[2:3]
    step = rr / rq
    norm = rr - 2.0 * step * rq + step * step * qq
    return norm, column_of(step), 1.0 + column_of(norm / rr)


def middle_kernel(
    way,
    parts_rows,
    parts_cols,
    cols,
    sums,
    starts,
    residuals,
    images,
    split_tiles,
    newton_tiles,
    diag,
    newton_diag,
    x_out,
    d_out,
    norm_out,
    keep,
    send,
    held,
    order,
    blocks,
    pieces,
):
    norm_out[...], step, grow = steps(sums)
    count = d_out.shape[0]
    for k, image in enumerate(images):
        r = residuals[k][...]
        x = starts[k][...] + step * r
        d = grow * r - step * image[...]
        if k == 0:
            x_out[...] = x
            d_out[...] = d
        held[k, 0:count], held[k, 3 * count : 4 * count] = split(x)
        held[k, count : 2 * count], held[k, 2 * count : 3 * count] = split(d)
    held[len(images)] = jnp.zeros(held.shape[1:], BF16)
    x1, d1 = x_out[...], d_out[...]
    found = seats(way, cols)

    def product(rows, tile):
        return lax.dot_general(rows, tile, NT, preferred_element_type=F32)

    first = second = None
    for seat, pair in zip(found, held_pairs(split_tiles)):
        block, (high, low) = held[seat], pair()
        one = product(block[count : 3 * count], high)
        two = product(block[count : 2 * count], low)
        first = one if first is None else first + one
        second = two if second is None else second + two
    own, (high, low) = held[0], split(diag[...] * 0.5)
    first += product(own[count : 3 * count], high)
    second += product(own[count : 2 * count], low)
    half_d = first[:count] + (first[count:] + second)
    curvature = 2.0 * row_sums(d1 * half_d)
    first = second = None
    for seat, pair in zip(found, held_pairs(newton_tiles)):
        block, (high, low) = held[seat], pair()
        one = product(block, high)
        two = product(block[: 2 * count], low)
        first = one if first is None else first + one
        second = two if second is None else second + two
    high, low = split(newton_diag[...] * 0.5)
    first += product(own, high)
    second += product(own[: 2 * count], low)
    ux = first[:count] + (first[3 * count :] + second[:count])
    ud = first[count : 2 * count] + (first[2 * count : 3 * count] + second[count:])
    hr, hc = count // parts_rows, count // parts_cols
    for r_index in range(parts_rows):
        for kind, pair in enumerate(((x1, ux), (d1, ud))):
            at = r_index * HALF + kind * hr
            for side in range(2):
                order[side, at : at + hr] = pair[side][
                    r_index * hr : (r_index + 1) * hr
                ]
        at = r_index * HALF + 2 * hr
        order[:, at : (r_index + 1) * HALF] = jnp.zeros(
            (2, HALF - 2 * hr, x1.shape[1]), F32
        )
    blocks[...] = dot_full(
        jnp.concatenate([x1, d1], axis=0), order[1], NT
    ) + dot_full(jnp.concatenate([ux, ud], axis=0), order[0], NT)
    depth = keep.shape[1]
    left = lax.broadcasted_iota(jnp.int32, (count, LANES), 1) < HALF
    wide = jnp.concatenate([curvature, jnp.zeros((1, LANES - count), F32)], axis=1)
    spot = lax.broadcasted_iota(jnp.int32, (depth, LANES), 0) == hc
    first_core = lax.axis_index("core") == 0
    for r_index in range(parts_rows):
        lanes = slice(r_index // 2 * LANES, (r_index // 2 + 1) * LANES)
        top, bottom = blocks[0:count, lanes], blocks[count : 2 * count, lanes]
        if r_index % 2:
            top = pltpu.roll(top, HALF, 1)
        else:
            bottom = pltpu.roll(bottom, HALF, 1)
        pieces[r_index, 0:count] = jnp.where(left, top, bottom)
        for pair in range(parts_cols // 2):
            one, two = (
                jnp.where(spot, wide, pieces[r_index, c * hc : c * hc + depth])
                for c in (2 * pair, 2 * pair + 1)
            )
            at = r_index * (parts_cols // 2) + pair
            keep[at] = jnp.where(first_core, one, two)
            send[at] = jnp.where(first_core, two, one)


def last_kernel(parts_rows, parts_cols, received, norm, x1, d1, x_out, hessian):
    total = received[0]
    for device in range(1, received.shape[0]):
        total = total + received[device]
    count = x1.shape[0]
    hr, hc = count // parts_rows, count // parts_cols
    step = norm[...] / total[hc : hc + 1, 0:count]
    step_col = column_of(step)
    x_out[...] = x1[...] + step_col * d1[...]
    row_at = lax.axis_index("row") * hr
    col_at = (lax.axis_index("chip") * 2 + lax.axis_index("core")) * hc
    wanted = lax.broadcasted_iota(jnp.int32, (count, hr), 0) == row_at + (
        lax.broadcasted_iota(jnp.int32, (count, hr), 1)
    )
    of_rows = jnp.sum(jnp.where(wanted, step_col, 0.0), axis=0, keepdims=True)
    wanted = lax.broadcasted_iota(jnp.int32, (hc, count), 1) == col_at + (
        lax.broadcasted_iota(jnp.int32, (hc, count), 0)
    )
    of_cols = jnp.sum(jnp.where(wanted, step, 0.0), axis=1, keepdims=True)
    xx = total[0:hc, 0:hr]
    dx = total[0:hc, hr : 2 * hr]
    xd = total[0:hc, HALF : HALF + hr]
    dd = total[0:hc, HALF + hr : HALF + 2 * hr]
    hessian[...] = xx + of_rows * dx + of_cols * (xd + of_rows * dd)


def on_device(
    precision_diag,
    precision_pairs,
    pattern_cols,
    newton_diag,
    newton_pairs,
    warm_start,
    target_rows,
):
    groups = lax.axis_size("row")
    chips = lax.axis_size("chip")
    columns = chips * 2
    count, size = warm_start.shape[1:]
    n = precision_pairs.shape[1]
    cols = pattern_cols[0]
    target = target_rows[None]
    tiles, diag = precision_pairs[0], precision_diag[0]
    ntiles, ndiag = newton_pairs[0], newton_diag[0]
    panel = (count, size)
    stack = (chips, count, size)
    swap = [(0, 1), (1, 0)]
    way = Way(chips)
    unit = 2 * count * size * size * 3
    parts = jax.ShapeDtypeStruct((2, n, size, size), BF16)
    work = (2 * chips + 1,) + panel
    held = jax.ShapeDtypeStruct((2 * chips + 1, 2 * count, size), BF16)

    def gather(value):
        same = [value] + [None] * (chips - 1)
        for k in range(1, chips):
            same[way.source(k)] = lax.ppermute(value, "chip", way.pairs(k))
        return same

    def forward(same):
        return list(same) + [lax.ppermute(block, "core", swap) for block in same]

    def scatter(keep, send):
        received = lax.ppermute(send, "core", swap)
        sums = [keep[k] + received[k] for k in range(chips)]
        added = [sums[0]]
        for k in range(1, chips):
            added.append(lax.ppermute(sums[k], "chip", way.pairs(k)))
        return added

    start = warm_start[0]
    starts = gather(start)
    keep, send, split_tiles = call(
        functools.partial(first_kernel, way),
        [stack, stack, parts],
        [],
        [Far(cols, pltpu.SMEM), Far(start), Far(tiles)],
        scratch=[work],
        flops=n * unit,
    )
    added = scatter(keep, send)
    starts = forward(starts)
    (base,) = call(diag_kernel, [panel], [], [start, diag], flops=2 * unit)
    residual, keep, send = call(
        functools.partial(residual_kernel, way),
        [panel, stack, stack],
        [cols],
        [base, target, starts, split_tiles, added],
        scratch=[work, held],
        flops=2 * n * unit,
    )
    residuals = gather(residual)
    added = scatter(keep, send)
    residuals = forward(residuals)
    base, newton_tiles = call(
        diag_split_kernel,
        [panel, parts],
        [],
        [residual, diag, ntiles],
        flops=4 * unit,
    )
    image, sums = call(
        functools.partial(image_kernel, way),
        [panel, (groups * columns, 3, count)],
        [cols],
        [residual, base, residuals, split_tiles, added],
        scratch=[held],
        flops=n * unit,
    )
    images = gather(image)
    sums = lax.all_to_all(sums, ALL, 0, 0, tiled=True)
    images = forward(images)
    hr, hc = count // groups, count // columns
    depth = -(-(hc + 1) // 8) * 8
    share = (groups * chips, depth, LANES)
    x1, d1, norm, keep, send = call(
        functools.partial(middle_kernel, way, groups, columns),
        [panel, panel, (1, count), share, share],
        [cols],
        [
            sums,
            starts,
            residuals,
            images,
            split_tiles,
            newton_tiles,
            diag,
            ndiag,
        ],
        scratch=[
            jax.ShapeDtypeStruct((2 * chips + 1, 4 * count, size), BF16),
            (2, groups * HALF, size),
            (2 * count, groups * HALF),
            (groups, count + depth, LANES),
        ],
        flops=4 * n * unit,
    )
    received = lax.ppermute(send, "core", swap)
    received = lax.all_to_all(keep + received, ("row", "chip"), 0, 0, tiled=True)
    solved, hessian = call(
        functools.partial(last_kernel, groups, columns),
        [panel, (hc, hr)],
        [],
        [received, norm, x1, d1],
        flops=unit // 100,
    )
    return solved[None], hessian.T


def solution(mesh):
    rows, columns = mesh.devices.shape
    fine = Mesh(mesh.devices.reshape(rows, columns // 2, 2), ALL)
    placed = (
        P(ALL, None, None),
        P(ALL, None, None, None),
        P(ALL, None),
        P(ALL, None, None),
        P(ALL, None, None, None),
        P(ALL, None, None),
        P(),
    )
    return jax.shard_map(
        on_device,
        mesh=fine,
        in_specs=placed,
        out_specs=(P(ALL, None, None), P("row", ("chip", "core"))),
        check_vma=False,
    )
```

```python
import functools

import jax
import jax.numpy as jnp
from jax import lax
from jax.experimental import pallas as pl
from jax.experimental.pallas import tpu as pltpu
from jax.sharding import Mesh, PartitionSpec as P


F32 = jnp.float32
BF16 = jnp.bfloat16
ALL = ("row", "chip", "core")
GRANT = 24 << 20
LANES = 128
HALF = 64

NT = (((1,), (1,)), ((), ()))
NN = (((1,), (0,)), ((), ()))


def split(value):
    high = value.astype(BF16)
    low = (value - high.astype(F32)).astype(BF16)
    return high, low


def dot3(left, right, dims):
    rows = left[0].shape[0]
    both = jnp.concatenate(left, axis=0)
    first = lax.dot_general(both, right[0], dims, preferred_element_type=F32)
    second = lax.dot_general(left[0], right[1], dims, preferred_element_type=F32)
    return first[:rows] + first[rows:] + second


def dot_full(left, right, dims):
    return lax.dot_general(
        left, right, dims, precision=lax.Precision.HIGHEST, preferred_element_type=F32
    )


def row_sums(product):
    return dot_full(jnp.ones((8, product.shape[1]), F32), product, NT)[0:1]


def column_of(row):
    n = row.shape[1]
    eye = lax.broadcasted_iota(jnp.int32, (n, n), 0) == lax.broadcasted_iota(
        jnp.int32, (n, n), 1
    )
    return jnp.sum(jnp.where(eye, row, 0.0), axis=1, keepdims=True)


class Far:
    def __init__(self, array, space=pltpu.VMEM):
        self.arrays = [pltpu.with_memory_space_constraint(array, pltpu.HBM)]
        self.pieces = array.shape[0] if array.ndim == 3 else 1
        self.buffer = space(array.shape, array.dtype)

    def copies(self, ref, buffer, sems):
        if self.pieces == 1:
            return [pltpu.make_async_copy(ref, buffer, sems.at[0])]
        return [
            pltpu.make_async_copy(ref.at[k], buffer.at[k], sems.at[k])
            for k in range(self.pieces)
        ]


class Fetched:
    def __init__(self, copies, ref):
        self.copies, self.ref, self.shape, self.done = copies, ref, ref.shape, 0

    def wait(self, upto=None):
        upto = len(self.copies) if upto is None else upto
        for k in range(self.done, upto):
            self.copies[k].wait()
        self.done = max(self.done, upto)
        return self.ref

    def all(self):
        return self.wait()[...]


def call(body, outs, scalars, operands, scratch=(), flops=0):
    flat, plan = [], []
    for one in operands:
        arrays = one.arrays if isinstance(one, Far) else one
        if not isinstance(arrays, (tuple, list)):
            arrays = [arrays]
        plan.append((one, len(flat), len(arrays)))
        flat.extend(arrays)
    fars = [one for one, _, _ in plan if isinstance(one, Far)]
    smem = pl.BlockSpec(memory_space=pltpu.SMEM)
    vmem = pl.BlockSpec(memory_space=pltpu.VMEM)
    specs = [smem] * len(scalars)
    for one, _, length in plan:
        specs += [pl.BlockSpec(memory_space=pl.ANY) if isinstance(one, Far) else vmem] * length

    def kernel(*refs):
        given, refs = refs[: len(scalars)], refs[len(scalars) :]
        arrays, refs = refs[: len(flat)], refs[len(flat) :]
        out, refs = refs[: len(outs)], refs[len(outs) :]
        mine, refs = refs[: len(scratch)], refs[len(scratch) :]
        buffers, sems = refs[: len(fars)], refs[len(fars) :]
        seen, at = [], 0
        for one, first, length in plan:
            if isinstance(one, Far):
                copies = one.copies(arrays[first], buffers[at], sems[at])
                for copy in copies:
                    copy.start()
                seen.append(Fetched(copies, buffers[at]))
                at += 1
            elif isinstance(one, (tuple, list)):
                seen.append(arrays[first : first + length])
            else:
                seen.append(arrays[first])
        body(*given, *seen, *out, *mine)

    outs = [o if isinstance(o, jax.ShapeDtypeStruct) else jax.ShapeDtypeStruct(o, F32) for o in outs]
    scratch = [o if isinstance(o, jax.ShapeDtypeStruct) else jax.ShapeDtypeStruct(o, F32) for o in scratch]
    return pl.pallas_call(
        kernel,
        out_shape=outs,
        in_specs=specs,
        out_specs=[vmem] * len(outs),
        scratch_shapes=[pltpu.VMEM(o.shape, o.dtype) for o in scratch]
        + [one.buffer for one in fars]
        + [pltpu.SemaphoreType.DMA((one.pieces,)) for one in fars],
        cost_estimate=pl.CostEstimate(
            flops=flops,
            bytes_accessed=sum(a.size * a.dtype.itemsize for a in flat),
            transcendentals=0,
        ),
        compiler_params=pltpu.CompilerParams(vmem_limit_bytes=GRANT),
    )(*scalars, *flat)


class Way:
    def __init__(self, chips):
        self.chips, self.power = chips, chips & (chips - 1) == 0

    def pairs(self, k):
        n = self.chips
        return [(i, i ^ k if self.power else (i + k) % n) for i in range(n)]

    def to(self, here, there):
        n = self.chips
        return there ^ here if self.power else lax.rem(there - here + n, n)

    def source(self, k):
        return k if self.power else (self.chips - k) % self.chips


def seats(way, cols):
    chip, core = lax.axis_index("chip"), lax.axis_index("core")
    first = lax.axis_index("row") * (2 * way.chips)
    found = []
    for k in range(cols.shape[0]):
        slot = jnp.maximum(cols[k] - first, 0)
        kind = jnp.where(lax.rem(slot, 2) == core, 0, way.chips)
        found.append(
            jnp.where(cols[k] >= 0, kind + way.to(chip, slot // 2), 2 * way.chips)
        )
    return found


def contributions(way, cols, pairs, panel, work, keep, send):
    chips = way.chips
    work[0 : 2 * chips] = jnp.zeros((2 * chips,) + work.shape[1:], F32)
    for seat, pair in zip(seats(way, cols), pairs):
        work[seat] = dot3(panel, pair(), NN)
    keep[...] = work[0:chips]
    send[...] = work[chips : 2 * chips]


def hold(gathered, held):
    for k, block in enumerate(gathered):
        high, low = split(block[...])
        rows = high.shape[0]
        held[k, 0:rows] = high
        held[k, rows : 2 * rows] = low
    held[len(gathered)] = jnp.zeros(held.shape[1:], BF16)


def off_diagonal(way, cols, pairs, held):
    rows = held.shape[1] // 2
    first = second = None
    for seat, pair in zip(seats(way, cols), pairs):
        both, (high, low) = held[seat], pair()
        one = lax.dot_general(both, high, NT, preferred_element_type=F32)
        two = lax.dot_general(both[:rows], low, NT, preferred_element_type=F32)
        first = one if first is None else first + one
        second = two if second is None else second + two
    return first[:rows] + (first[rows:] + second)


def held_pairs(split_tiles):
    return [
        functools.partial(lambda k: (split_tiles[0, k], split_tiles[1, k]), k)
        for k in range(split_tiles.shape[1])
    ]


def first_kernel(way, cols, panel, tiles, keep, send, split_tiles, work):
    cols = cols.wait()
    n = split_tiles.shape[1]

    def pair(k):
        if k in (0, (n + 1) // 2):
            tiles.wait(n if k else (n + 1) // 2)
        high, low = split(tiles.ref[k])
        split_tiles[0, k], split_tiles[1, k] = high, low
        return high, low

    pairs = [functools.partial(pair, k) for k in range(n)]
    contributions(way, cols, pairs, split(panel.all()), work, keep, send)


def diag_kernel(panel, diag, image):
    image[...] = dot_full(panel[...], diag.all(), NT)


def residual_kernel(
    way, cols, base, target, gathered, split_tiles, added, residual, keep, send, work, held
):
    pairs = held_pairs(split_tiles)
    hold(gathered, held)
    total = base[...] + off_diagonal(way, cols, pairs, held)
    for block in added:
        total = total + block[...]
    rows, size = residual.shape
    chips = way.chips
    block = (lax.axis_index("row") * chips + lax.axis_index("chip")) * 2
    block = block + lax.axis_index("core")
    at = column_of((target[...] - block * size).astype(F32))
    unit = at == lax.broadcasted_iota(jnp.int32, (rows, size), 1).astype(F32)
    value = unit.astype(F32) - total
    residual[...] = value
    contributions(way, cols, pairs, split(value), work, keep, send)


def image_kernel(
    way, cols, panel, base, gathered, split_tiles, added, image, half, sums, held
):
    hold(gathered, held)
    off = off_diagonal(way, cols, held_pairs(split_tiles), held)
    half[...] = off + 0.5 * base[...]
    total = off + base[...]
    for block in added:
        total = total + block[...]
    image[...] = total
    value = panel[...]
    found = jnp.concatenate(
        [row_sums(value * value), row_sums(value * total), row_sums(total * total)], 0
    )
    sums[...] = jnp.broadcast_to(found[None], sums.shape)


def steps(sums):
    totals = sums[0]
    for device in range(1, sums.shape[0]):
        totals = totals + sums[device]
    rr, rq, qq = totals[0:1], totals[1:2], totals[2:3]
    step = rr / rq
    norm = rr - 2.0 * step * rq + step * step * qq
    return norm, column_of(step), 1.0 + column_of(norm / rr)


def newton_kernel(way, cols, gathered, diag, tiles, out, *more):
    *split_tiles, held = more
    rows = out.shape[0]
    for k, block in enumerate(gathered):
        value = block[...]
        high, rest = split(value)
        middle = value - high.astype(F32)
        held[k, 0:rows], held[k, rows : 2 * rows] = high, rest
        held[k, 2 * rows : 3 * rows] = (middle - rest.astype(F32)).astype(BF16)
    held[len(gathered)] = jnp.zeros(held.shape[1:], BF16)
    first = second = None
    work = [(seat, tiles[k]) for k, seat in enumerate(seats(way, cols))]
    for k, (seat, tile) in enumerate(work + [(0, None)]):
        three = held[seat]
        high, low = split(diag.all() * 0.5 if tile is None else tile)
        if tile is not None and split_tiles:
            split_tiles[0][0, k], split_tiles[0][1, k] = high, low
        one = lax.dot_general(three, high, NT, preferred_element_type=F32)
        two = lax.dot_general(three[: 2 * rows], low, NT, preferred_element_type=F32)
        first = one if first is None else first + one
        second = two if second is None else second + two
    small = first[2 * rows :] + second[rows:]
    out[...] = first[:rows] + (first[rows : 2 * rows] + second[:rows] + small)


def half_product(both, pair):
    rows = both.shape[0] // 2
    one = lax.dot_general(both, pair[0], NT, preferred_element_type=F32)
    two = lax.dot_general(both[:rows], pair[1], NT, preferred_element_type=F32)
    return one[:rows] + (one[rows:] + two)


def whole_pairs(tiles):
    return [
        functools.partial(lambda k: split(tiles[k]), k) for k in range(tiles.shape[0])
    ]


def halves_kernel(
    way, cols, images, tiles, newton_tiles, diag, newton_diag, half, newton, held
):
    hold(images, held)
    first = off_diagonal(way, cols, whole_pairs(tiles), held)
    second = off_diagonal(way, cols, held_pairs(newton_tiles), held)
    half[...] = first + half_product(held[0], split(diag.all() * 0.5))
    newton[...] = second + half_product(held[0], split(newton_diag.all() * 0.5))


def middle_kernel(
    parts_rows,
    parts_cols,
    sums,
    start,
    residual,
    image,
    half_residual,
    half_image,
    newton_start,
    newton_residual,
    newton_image,
    x_out,
    d_out,
    norm_out,
    keep,
    send,
    order,
    blocks,
    pieces,
):
    norm_out[...], step, grow = steps(sums)
    count = d_out.shape[0]
    r, q = residual[...], image[...]
    x1 = start[...] + step * r
    d1 = grow * r - step * q
    x_out[...] = x1
    d_out[...] = d1
    half_d = grow * half_residual[...] - step * half_image[...]
    curvature = 2.0 * row_sums(d1 * half_d)
    ux = newton_start[...] + step * newton_residual[...]
    ud = grow * newton_residual[...] - step * newton_image[...]
    hr, hc = count // parts_rows, count // parts_cols
    for r_index in range(parts_rows):
        for kind, pair in enumerate(((x1, ux), (d1, ud))):
            at = r_index * HALF + kind * hr
            for side in range(2):
                order[side, at : at + hr] = pair[side][
                    r_index * hr : (r_index + 1) * hr
                ]
        at = r_index * HALF + 2 * hr
        order[:, at : (r_index + 1) * HALF] = jnp.zeros(
            (2, HALF - 2 * hr, x1.shape[1]), F32
        )
    blocks[...] = dot_full(
        jnp.concatenate([x1, d1], axis=0), order[1], NT
    ) + dot_full(jnp.concatenate([ux, ud], axis=0), order[0], NT)
    depth = keep.shape[1]
    left = lax.broadcasted_iota(jnp.int32, (count, LANES), 1) < HALF
    wide = jnp.concatenate([curvature, jnp.zeros((1, LANES - count), F32)], axis=1)
    spot = lax.broadcasted_iota(jnp.int32, (depth, LANES), 0) == hc
    first_core = lax.axis_index("core") == 0
    for r_index in range(parts_rows):
        lanes = slice(r_index // 2 * LANES, (r_index // 2 + 1) * LANES)
        top, bottom = blocks[0:count, lanes], blocks[count : 2 * count, lanes]
        if r_index % 2:
            top = pltpu.roll(top, HALF, 1)
        else:
            bottom = pltpu.roll(bottom, HALF, 1)
        pieces[r_index, 0:count] = jnp.where(left, top, bottom)
        for pair in range(parts_cols // 2):
            one, two = (
                jnp.where(spot, wide, pieces[r_index, c * hc : c * hc + depth])
                for c in (2 * pair, 2 * pair + 1)
            )
            at = r_index * (parts_cols // 2) + pair
            keep[at] = jnp.where(first_core, one, two)
            send[at] = jnp.where(first_core, two, one)


def last_kernel(parts_rows, parts_cols, received, norm, x1, d1, x_out, hessian):
    total = received[0]
    for device in range(1, received.shape[0]):
        total = total + received[device]
    count = x1.shape[0]
    hr, hc = count // parts_rows, count // parts_cols
    step = norm[...] / total[hc : hc + 1, 0:count]
    step_col = column_of(step)
    x_out[...] = x1[...] + step_col * d1[...]
    row_at = lax.axis_index("row") * hr
    col_at = (lax.axis_index("chip") * 2 + lax.axis_index("core")) * hc
    wanted = lax.broadcasted_iota(jnp.int32, (count, hr), 0) == row_at + (
        lax.broadcasted_iota(jnp.int32, (count, hr), 1)
    )
    of_rows = jnp.sum(jnp.where(wanted, step_col, 0.0), axis=0, keepdims=True)
    wanted = lax.broadcasted_iota(jnp.int32, (hc, count), 1) == col_at + (
        lax.broadcasted_iota(jnp.int32, (hc, count), 0)
    )
    of_cols = jnp.sum(jnp.where(wanted, step, 0.0), axis=1, keepdims=True)
    xx = total[0:hc, 0:hr]
    dx = total[0:hc, hr : 2 * hr]
    xd = total[0:hc, HALF : HALF + hr]
    dd = total[0:hc, HALF + hr : HALF + 2 * hr]
    hessian[...] = xx + of_rows * dx + of_cols * (xd + of_rows * dd)


def on_device(
    precision_diag,
    precision_pairs,
    pattern_cols,
    newton_diag,
    newton_pairs,
    warm_start,
    target_rows,
):
    groups = lax.axis_size("row")
    chips = lax.axis_size("chip")
    columns = chips * 2
    count, size = warm_start.shape[1:]
    n = precision_pairs.shape[1]
    cols = pattern_cols[0]
    target = target_rows[None]
    tiles, diag = precision_pairs[0], precision_diag[0]
    ntiles, ndiag = newton_pairs[0], newton_diag[0]
    panel = (count, size)
    stack = (chips, count, size)
    swap = [(0, 1), (1, 0)]
    way = Way(chips)
    unit = 2 * count * size * size * 3
    parts = jax.ShapeDtypeStruct((2, n, size, size), BF16)
    work = (2 * chips + 1,) + panel
    held = jax.ShapeDtypeStruct((2 * chips + 1, 2 * count, size), BF16)

    def gather(value):
        same = [value] + [None] * (chips - 1)
        for k in range(1, chips):
            same[way.source(k)] = lax.ppermute(value, "chip", way.pairs(k))
        return same

    def forward(same):
        return list(same) + [lax.ppermute(block, "core", swap) for block in same]

    def scatter(keep, send):
        received = lax.ppermute(send, "core", swap)
        sums = [keep[k] + received[k] for k in range(chips)]
        added = [sums[0]]
        for k in range(1, chips):
            added.append(lax.ppermute(sums[k], "chip", way.pairs(k)))
        return added

    start = warm_start[0]
    starts = gather(start)
    keep, send, split_tiles = call(
        functools.partial(first_kernel, way),
        [stack, stack, parts],
        [],
        [Far(cols, pltpu.SMEM), Far(start), Far(tiles)],
        scratch=[work],
        flops=n * unit,
    )
    added = scatter(keep, send)
    starts = forward(starts)
    (base,) = call(diag_kernel, [panel], [], [start, Far(diag)], flops=2 * unit)
    residual, keep, send = call(
        functools.partial(residual_kernel, way),
        [panel, stack, stack],
        [cols],
        [base, target, starts, split_tiles, added],
        scratch=[work, held],
        flops=2 * n * unit,
    )
    residuals = gather(residual)
    added = scatter(keep, send)
    residuals = forward(residuals)
    (base,) = call(diag_kernel, [panel], [], [residual, Far(diag)], flops=2 * unit)

    def newton_half(gathered, phase):
        return call(
            functools.partial(newton_kernel, way),
            [panel, parts][: phase + 1],
            [cols],
            [gathered, Far(ndiag), ntiles],
            scratch=[
                jax.ShapeDtypeStruct((2 * chips + 1, 3 * count, size), BF16)
            ],
            flops=2 * n * unit,
        )

    (newton_start,) = newton_half(starts, 0)
    newton_residual, newton_tiles = newton_half(residuals, 1)
    image, half_residual, sums = call(
        functools.partial(image_kernel, way),
        [panel, panel, (groups * columns, 3, count)],
        [cols],
        [residual, base, residuals, split_tiles, added],
        scratch=[held],
        flops=n * unit,
    )
    images = gather(image)
    sums = lax.all_to_all(sums, ALL, 0, 0, tiled=True)
    images = forward(images)
    hr, hc = count // groups, count // columns
    depth = -(-(hc + 1) // 8) * 8
    share = (groups * chips, depth, LANES)
    half_image, newton_image = call(
        functools.partial(halves_kernel, way),
        [panel, panel],
        [cols],
        [images, tiles, newton_tiles, Far(diag), Far(ndiag)],
        scratch=[held],
        flops=2 * n * unit,
    )
    x1, d1, norm, keep, send = call(
        functools.partial(middle_kernel, groups, columns),
        [panel, panel, (1, count), share, share],
        [],
        [
            sums,
            start,
            residual,
            image,
            half_residual,
            half_image,
            newton_start,
            newton_residual,
            newton_image,
        ],
        scratch=[
            (2, groups * HALF, size),
            (2 * count, groups * HALF),
            (groups, count + depth, LANES),
        ],
        flops=n * unit,
    )
    received = lax.ppermute(send, "core", swap)
    received = lax.all_to_all(keep + received, ("row", "chip"), 0, 0, tiled=True)
    solved, hessian = call(
        functools.partial(last_kernel, groups, columns),
        [panel, (hc, hr)],
        [],
        [received, norm, x1, d1],
        flops=unit // 100,
    )
    return solved[None], hessian.T


def solution(mesh):
    rows, columns = mesh.devices.shape
    fine = Mesh(mesh.devices.reshape(rows, columns // 2, 2), ALL)
    placed = (
        P(ALL, None, None),
        P(ALL, None, None, None),
        P(ALL, None),
        P(ALL, None, None),
        P(ALL, None, None, None),
        P(ALL, None, None),
        P(),
    )
    return jax.shard_map(
        on_device,
        mesh=fine,
        in_specs=placed,
        out_specs=(P(ALL, None, None), P("row", ("chip", "core"))),
        check_vma=False,
    )
```

```python
import functools

import jax
import jax.numpy as jnp
from jax import lax
from jax.experimental import pallas as pl
from jax.experimental.pallas import tpu as pltpu
from jax.sharding import Mesh, PartitionSpec as P


F32 = jnp.float32
BF16 = jnp.bfloat16
ALL = ("row", "chip", "core")
GRANT = 24 << 20
LANES = 128
HALF = 64

NT = (((1,), (1,)), ((), ()))
NN = (((1,), (0,)), ((), ()))


def split(value):
    high = value.astype(BF16)
    low = (value - high.astype(F32)).astype(BF16)
    return high, low


def dot3(left, right, dims):
    rows = left[0].shape[0]
    both = jnp.concatenate(left, axis=0)
    first = lax.dot_general(both, right[0], dims, preferred_element_type=F32)
    second = lax.dot_general(left[0], right[1], dims, preferred_element_type=F32)
    return first[:rows] + first[rows:] + second


def dot_full(left, right, dims):
    return lax.dot_general(
        left, right, dims, precision=lax.Precision.HIGHEST, preferred_element_type=F32
    )


def row_sums(product):
    return dot_full(jnp.ones((8, product.shape[1]), F32), product, NT)[0:1]


def column_of(row):
    n = row.shape[1]
    eye = lax.broadcasted_iota(jnp.int32, (n, n), 0) == lax.broadcasted_iota(
        jnp.int32, (n, n), 1
    )
    return jnp.sum(jnp.where(eye, row, 0.0), axis=1, keepdims=True)


class Far:
    def __init__(self, array, space=pltpu.VMEM):
        self.arrays = [pltpu.with_memory_space_constraint(array, pltpu.HBM)]
        self.pieces = array.shape[0] if array.ndim == 3 else 1
        self.buffer = space(array.shape, array.dtype)

    def copies(self, ref, buffer, sems):
        if self.pieces == 1:
            return [pltpu.make_async_copy(ref, buffer, sems.at[0])]
        return [
            pltpu.make_async_copy(ref.at[k], buffer.at[k], sems.at[k])
            for k in range(self.pieces)
        ]


class Fetched:
    def __init__(self, copies, ref):
        self.copies, self.ref, self.shape, self.done = copies, ref, ref.shape, 0

    def wait(self, upto=None):
        upto = len(self.copies) if upto is None else upto
        for k in range(self.done, upto):
            self.copies[k].wait()
        self.done = max(self.done, upto)
        return self.ref

    def all(self):
        return self.wait()[...]


def call(body, outs, scalars, operands, scratch=(), flops=0):
    flat, plan = [], []
    for one in operands:
        arrays = one.arrays if isinstance(one, Far) else one
        if not isinstance(arrays, (tuple, list)):
            arrays = [arrays]
        plan.append((one, len(flat), len(arrays)))
        flat.extend(arrays)
    fars = [one for one, _, _ in plan if isinstance(one, Far)]
    smem = pl.BlockSpec(memory_space=pltpu.SMEM)
    vmem = pl.BlockSpec(memory_space=pltpu.VMEM)
    specs = [smem] * len(scalars)
    for one, _, length in plan:
        specs += [pl.BlockSpec(memory_space=pl.ANY) if isinstance(one, Far) else vmem] * length

    def kernel(*refs):
        given, refs = refs[: len(scalars)], refs[len(scalars) :]
        arrays, refs = refs[: len(flat)], refs[len(flat) :]
        out, refs = refs[: len(outs)], refs[len(outs) :]
        mine, refs = refs[: len(scratch)], refs[len(scratch) :]
        buffers, sems = refs[: len(fars)], refs[len(fars) :]
        seen, at = [], 0
        for one, first, length in plan:
            if isinstance(one, Far):
                copies = one.copies(arrays[first], buffers[at], sems[at])
                for copy in copies:
                    copy.start()
                seen.append(Fetched(copies, buffers[at]))
                at += 1
            elif isinstance(one, (tuple, list)):
                seen.append(arrays[first : first + length])
            else:
                seen.append(arrays[first])
        body(*given, *seen, *out, *mine)

    outs = [o if isinstance(o, jax.ShapeDtypeStruct) else jax.ShapeDtypeStruct(o, F32) for o in outs]
    scratch = [o if isinstance(o, jax.ShapeDtypeStruct) else jax.ShapeDtypeStruct(o, F32) for o in scratch]
    return pl.pallas_call(
        kernel,
        out_shape=outs,
        in_specs=specs,
        out_specs=[vmem] * len(outs),
        scratch_shapes=[pltpu.VMEM(o.shape, o.dtype) for o in scratch]
        + [one.buffer for one in fars]
        + [pltpu.SemaphoreType.DMA((one.pieces,)) for one in fars],
        cost_estimate=pl.CostEstimate(
            flops=flops,
            bytes_accessed=sum(a.size * a.dtype.itemsize for a in flat),
            transcendentals=0,
        ),
        compiler_params=pltpu.CompilerParams(vmem_limit_bytes=GRANT),
    )(*scalars, *flat)


class Way:
    def __init__(self, chips):
        self.chips, self.power = chips, chips & (chips - 1) == 0

    def pairs(self, k):
        n = self.chips
        return [(i, i ^ k if self.power else (i + k) % n) for i in range(n)]

    def to(self, here, there):
        n = self.chips
        return there ^ here if self.power else lax.rem(there - here + n, n)

    def source(self, k):
        return k if self.power else (self.chips - k) % self.chips


def seats(way, cols):
    chip, core = lax.axis_index("chip"), lax.axis_index("core")
    first = lax.axis_index("row") * (2 * way.chips)
    found = []
    for k in range(cols.shape[0]):
        slot = jnp.maximum(cols[k] - first, 0)
        kind = jnp.where(lax.rem(slot, 2) == core, 0, way.chips)
        found.append(
            jnp.where(cols[k] >= 0, kind + way.to(chip, slot // 2), 2 * way.chips)
        )
    return found


def contributions(way, cols, pairs, panel, work, keep, send):
    chips = way.chips
    work[0 : 2 * chips] = jnp.zeros((2 * chips,) + work.shape[1:], F32)
    for seat, pair in zip(seats(way, cols), pairs):
        work[seat] = dot3(panel, pair(), NN)
    keep[...] = work[0:chips]
    send[...] = work[chips : 2 * chips]


def hold(gathered, held):
    for k, block in enumerate(gathered):
        high, low = split(block[...])
        rows = high.shape[0]
        held[k, 0:rows] = high
        held[k, rows : 2 * rows] = low
    held[len(gathered)] = jnp.zeros(held.shape[1:], BF16)


def off_diagonal(way, cols, pairs, held):
    rows = held.shape[1] // 2
    first = second = None
    for seat, pair in zip(seats(way, cols), pairs):
        both, (high, low) = held[seat], pair()
        one = lax.dot_general(both, high, NT, preferred_element_type=F32)
        two = lax.dot_general(both[:rows], low, NT, preferred_element_type=F32)
        first = one if first is None else first + one
        second = two if second is None else second + two
    return first[:rows] + (first[rows:] + second)


def held_pairs(split_tiles):
    return [
        functools.partial(lambda k: (split_tiles[0, k], split_tiles[1, k]), k)
        for k in range(split_tiles.shape[1])
    ]


def first_kernel(way, cols, panel, tiles, keep, send, split_tiles, work):
    cols = cols.wait()
    n = split_tiles.shape[1]

    def pair(k):
        if k in (0, (n + 1) // 2):
            tiles.wait(n if k else (n + 1) // 2)
        high, low = split(tiles.ref[k])
        split_tiles[0, k], split_tiles[1, k] = high, low
        return high, low

    pairs = [functools.partial(pair, k) for k in range(n)]
    contributions(way, cols, pairs, split(panel.all()), work, keep, send)


def diag_kernel(panel, diag, image):
    image[...] = dot_full(panel[...], diag[...], NT)


def off_kernel(way, cols, gathered, split_tiles, out, held):
    hold(gathered, held)
    out[...] = off_diagonal(way, cols, held_pairs(split_tiles), held)


def residual_kernel(
    way, cols, base, off, target, split_tiles, added, residual, keep, send, work
):
    total = base[...] + off[...]
    for block in added:
        total = total + block[...]
    rows, size = residual.shape
    chips = way.chips
    block = (lax.axis_index("row") * chips + lax.axis_index("chip")) * 2
    block = block + lax.axis_index("core")
    at = column_of((target[...] - block * size).astype(F32))
    unit = at == lax.broadcasted_iota(jnp.int32, (rows, size), 1).astype(F32)
    value = unit.astype(F32) - total
    residual[...] = value
    contributions(way, cols, held_pairs(split_tiles), split(value), work, keep, send)


def image_kernel(panel, base, off, added, image, half, sums):
    half[...] = off[...] + 0.5 * base[...]
    total = off[...] + base[...]
    for block in added:
        total = total + block[...]
    image[...] = total
    value = panel[...]
    found = jnp.concatenate(
        [row_sums(value * value), row_sums(value * total), row_sums(total * total)], 0
    )
    sums[...] = jnp.broadcast_to(found[None], sums.shape)


def steps(sums):
    totals = sums[0]
    for device in range(1, sums.shape[0]):
        totals = totals + sums[device]
    rr, rq, qq = totals[0:1], totals[1:2], totals[2:3]
    step = rr / rq
    norm = rr - 2.0 * step * rq + step * step * qq
    return norm, column_of(step), 1.0 + column_of(norm / rr)


def newton_kernel(way, cols, gathered, diag, tiles, out, *more):
    *split_tiles, held = more
    rows = out.shape[0]
    for k, block in enumerate(gathered):
        value = block[...]
        high, rest = split(value)
        middle = value - high.astype(F32)
        held[k, 0:rows], held[k, rows : 2 * rows] = high, rest
        held[k, 2 * rows : 3 * rows] = (middle - rest.astype(F32)).astype(BF16)
    held[len(gathered)] = jnp.zeros(held.shape[1:], BF16)
    first = second = None
    work = [(seat, tiles[k]) for k, seat in enumerate(seats(way, cols))]
    for k, (seat, tile) in enumerate(work + [(0, None)]):
        three = held[seat]
        high, low = split(diag.all() * 0.5 if tile is None else tile)
        if tile is not None and split_tiles:
            split_tiles[0][0, k], split_tiles[0][1, k] = high, low
        one = lax.dot_general(three, high, NT, preferred_element_type=F32)
        two = lax.dot_general(three[: 2 * rows], low, NT, preferred_element_type=F32)
        first = one if first is None else first + one
        second = two if second is None else second + two
    small = first[2 * rows :] + second[rows:]
    out[...] = first[:rows] + (first[rows : 2 * rows] + second[:rows] + small)


def half_product(both, pair):
    rows = both.shape[0] // 2
    one = lax.dot_general(both, pair[0], NT, preferred_element_type=F32)
    two = lax.dot_general(both[:rows], pair[1], NT, preferred_element_type=F32)
    return one[:rows] + (one[rows:] + two)


def whole_pairs(tiles):
    return [
        functools.partial(lambda k: split(tiles[k]), k) for k in range(tiles.shape[0])
    ]


def halves_kernel(
    way, cols, images, tiles, newton_tiles, diag, newton_diag, half, newton, held
):
    hold(images, held)
    first = off_diagonal(way, cols, whole_pairs(tiles), held)
    second = off_diagonal(way, cols, held_pairs(newton_tiles), held)
    half[...] = first + half_product(held[0], split(diag.all() * 0.5))
    newton[...] = second + half_product(held[0], split(newton_diag.all() * 0.5))


def middle_kernel(
    parts_rows,
    parts_cols,
    sums,
    start,
    residual,
    image,
    half_residual,
    half_image,
    newton_start,
    newton_residual,
    newton_image,
    x_out,
    d_out,
    norm_out,
    keep,
    send,
    order,
    blocks,
    pieces,
):
    norm_out[...], step, grow = steps(sums)
    count = d_out.shape[0]
    r, q = residual[...], image[...]
    x1 = start[...] + step * r
    d1 = grow * r - step * q
    x_out[...] = x1
    d_out[...] = d1
    half_d = grow * half_residual[...] - step * half_image[...]
    curvature = 2.0 * row_sums(d1 * half_d)
    ux = newton_start[...] + step * newton_residual[...]
    ud = grow * newton_residual[...] - step * newton_image[...]
    hr, hc = count // parts_rows, count // parts_cols
    for r_index in range(parts_rows):
        for kind, pair in enumerate(((x1, ux), (d1, ud))):
            at = r_index * HALF + kind * hr
            for side in range(2):
                order[side, at : at + hr] = pair[side][
                    r_index * hr : (r_index + 1) * hr
                ]
        at = r_index * HALF + 2 * hr
        order[:, at : (r_index + 1) * HALF] = jnp.zeros(
            (2, HALF - 2 * hr, x1.shape[1]), F32
        )
    blocks[...] = dot_full(
        jnp.concatenate([x1, d1], axis=0), order[1], NT
    ) + dot_full(jnp.concatenate([ux, ud], axis=0), order[0], NT)
    depth = keep.shape[1]
    left = lax.broadcasted_iota(jnp.int32, (count, LANES), 1) < HALF
    wide = jnp.concatenate([curvature, jnp.zeros((1, LANES - count), F32)], axis=1)
    spot = lax.broadcasted_iota(jnp.int32, (depth, LANES), 0) == hc
    first_core = lax.axis_index("core") == 0
    for r_index in range(parts_rows):
        lanes = slice(r_index // 2 * LANES, (r_index // 2 + 1) * LANES)
        top, bottom = blocks[0:count, lanes], blocks[count : 2 * count, lanes]
        if r_index % 2:
            top = pltpu.roll(top, HALF, 1)
        else:
            bottom = pltpu.roll(bottom, HALF, 1)
        pieces[r_index, 0:count] = jnp.where(left, top, bottom)
        for pair in range(parts_cols // 2):
            one, two = (
                jnp.where(spot, wide, pieces[r_index, c * hc : c * hc + depth])
                for c in (2 * pair, 2 * pair + 1)
            )
            at = r_index * (parts_cols // 2) + pair
            keep[at] = jnp.where(first_core, one, two)
            send[at] = jnp.where(first_core, two, one)


def last_kernel(parts_rows, parts_cols, received, norm, x1, d1, x_out, hessian):
    total = received[0]
    for device in range(1, received.shape[0]):
        total = total + received[device]
    count = x1.shape[0]
    hr, hc = count // parts_rows, count // parts_cols
    step = norm[...] / total[hc : hc + 1, 0:count]
    step_col = column_of(step)
    x_out[...] = x1[...] + step_col * d1[...]
    row_at = lax.axis_index("row") * hr
    col_at = (lax.axis_index("chip") * 2 + lax.axis_index("core")) * hc
    wanted = lax.broadcasted_iota(jnp.int32, (count, hr), 0) == row_at + (
        lax.broadcasted_iota(jnp.int32, (count, hr), 1)
    )
    of_rows = jnp.sum(jnp.where(wanted, step_col, 0.0), axis=0, keepdims=True)
    wanted = lax.broadcasted_iota(jnp.int32, (hc, count), 1) == col_at + (
        lax.broadcasted_iota(jnp.int32, (hc, count), 0)
    )
    of_cols = jnp.sum(jnp.where(wanted, step, 0.0), axis=1, keepdims=True)
    xx = total[0:hc, 0:hr]
    dx = total[0:hc, hr : 2 * hr]
    xd = total[0:hc, HALF : HALF + hr]
    dd = total[0:hc, HALF + hr : HALF + 2 * hr]
    hessian[...] = xx + of_rows * dx + of_cols * (xd + of_rows * dd)


def on_device(
    precision_diag,
    precision_pairs,
    pattern_cols,
    newton_diag,
    newton_pairs,
    warm_start,
    target_rows,
):
    groups = lax.axis_size("row")
    chips = lax.axis_size("chip")
    columns = chips * 2
    count, size = warm_start.shape[1:]
    n = precision_pairs.shape[1]
    cols = pattern_cols[0]
    target = target_rows[None]
    tiles, diag = precision_pairs[0], precision_diag[0]
    ntiles, ndiag = newton_pairs[0], newton_diag[0]
    panel = (count, size)
    stack = (chips, count, size)
    swap = [(0, 1), (1, 0)]
    way = Way(chips)
    unit = 2 * count * size * size * 3
    parts = jax.ShapeDtypeStruct((2, n, size, size), BF16)
    work = (2 * chips + 1,) + panel
    held = jax.ShapeDtypeStruct((2 * chips + 1, 2 * count, size), BF16)

    def gather(value):
        same = [value] + [None] * (chips - 1)
        for k in range(1, chips):
            same[way.source(k)] = lax.ppermute(value, "chip", way.pairs(k))
        return same

    def forward(same):
        return list(same) + [lax.ppermute(block, "core", swap) for block in same]

    def scatter(keep, send):
        received = lax.ppermute(send, "core", swap)
        sums = [keep[k] + received[k] for k in range(chips)]
        added = [sums[0]]
        for k in range(1, chips):
            added.append(lax.ppermute(sums[k], "chip", way.pairs(k)))
        return added

    start = warm_start[0]
    starts = gather(start)
    keep, send, split_tiles = call(
        functools.partial(first_kernel, way),
        [stack, stack, parts],
        [],
        [Far(cols, pltpu.SMEM), Far(start), Far(tiles)],
        scratch=[work],
        flops=n * unit,
    )
    added = scatter(keep, send)
    starts = forward(starts)
    (base,) = call(diag_kernel, [panel], [], [start, diag], flops=2 * unit)

    def off_half(gathered):
        return call(
            functools.partial(off_kernel, way),
            [panel],
            [cols],
            [gathered, split_tiles],
            scratch=[held],
            flops=n * unit,
        )[0]

    residual, keep, send = call(
        functools.partial(residual_kernel, way),
        [panel, stack, stack],
        [cols],
        [base, off_half(starts), target, split_tiles, added],
        scratch=[work],
        flops=n * unit,
    )
    residuals = gather(residual)
    added = scatter(keep, send)
    residuals = forward(residuals)
    (base,) = call(diag_kernel, [panel], [], [residual, diag], flops=2 * unit)

    def newton_half(gathered, phase):
        return call(
            functools.partial(newton_kernel, way),
            [panel, parts][: phase + 1],
            [cols],
            [gathered, Far(ndiag), ntiles],
            scratch=[
                jax.ShapeDtypeStruct((2 * chips + 1, 3 * count, size), BF16)
            ],
            flops=2 * n * unit,
        )

    (newton_start,) = newton_half(starts, 0)
    newton_residual, newton_tiles = newton_half(residuals, 1)
    image, half_residual, sums = call(
        image_kernel,
        [panel, panel, (groups * columns, 3, count)],
        [],
        [residual, base, off_half(residuals), added],
        flops=unit // 10,
    )
    images = gather(image)
    sums = lax.all_to_all(sums, ALL, 0, 0, tiled=True)
    images = forward(images)
    hr, hc = count // groups, count // columns
    depth = -(-(hc + 1) // 8) * 8
    share = (groups * chips, depth, LANES)
    half_image, newton_image = call(
        functools.partial(halves_kernel, way),
        [panel, panel],
        [cols],
        [images, tiles, newton_tiles, Far(diag), Far(ndiag)],
        scratch=[held],
        flops=2 * n * unit,
    )
    x1, d1, norm, keep, send = call(
        functools.partial(middle_kernel, groups, columns),
        [panel, panel, (1, count), share, share],
        [],
        [
            sums,
            start,
            residual,
            image,
            half_residual,
            half_image,
            newton_start,
            newton_residual,
            newton_image,
        ],
        scratch=[
            (2, groups * HALF, size),
            (2 * count, groups * HALF),
            (groups, count + depth, LANES),
        ],
        flops=n * unit,
    )
    received = lax.ppermute(send, "core", swap)
    received = lax.all_to_all(keep + received, ("row", "chip"), 0, 0, tiled=True)
    solved, hessian = call(
        functools.partial(last_kernel, groups, columns),
        [panel, (hc, hr)],
        [],
        [received, norm, x1, d1],
        flops=unit // 100,
    )
    return solved[None], hessian.T


def solution(mesh):
    rows, columns = mesh.devices.shape
    fine = Mesh(mesh.devices.reshape(rows, columns // 2, 2), ALL)
    placed = (
        P(ALL, None, None),
        P(ALL, None, None, None),
        P(ALL, None),
        P(ALL, None, None),
        P(ALL, None, None, None),
        P(ALL, None, None),
        P(),
    )
    return jax.shard_map(
        on_device,
        mesh=fine,
        in_specs=placed,
        out_specs=(P(ALL, None, None), P("row", ("chip", "core"))),
        check_vma=False,
    )
```

```python
import functools

import jax
import jax.numpy as jnp
from jax import lax
from jax.experimental import pallas as pl
from jax.experimental.pallas import tpu as pltpu
from jax.sharding import Mesh, PartitionSpec as P


F32 = jnp.float32
BF16 = jnp.bfloat16
ALL = ("row", "chip", "core")
GRANT = 24 << 20
LANES = 128
HALF = 64

NT = (((1,), (1,)), ((), ()))
NN = (((1,), (0,)), ((), ()))


def split(value):
    high = value.astype(BF16)
    low = (value - high.astype(F32)).astype(BF16)
    return high, low


def dot3(left, right, dims):
    rows = left[0].shape[0]
    both = jnp.concatenate(left, axis=0)
    first = lax.dot_general(both, right[0], dims, preferred_element_type=F32)
    second = lax.dot_general(left[0], right[1], dims, preferred_element_type=F32)
    return first[:rows] + first[rows:] + second


def dot_full(left, right, dims):
    return lax.dot_general(
        left, right, dims, precision=lax.Precision.HIGHEST, preferred_element_type=F32
    )


def row_sums(product):
    return dot_full(jnp.ones((8, product.shape[1]), F32), product, NT)[0:1]


def column_of(row):
    n = row.shape[1]
    eye = lax.broadcasted_iota(jnp.int32, (n, n), 0) == lax.broadcasted_iota(
        jnp.int32, (n, n), 1
    )
    return jnp.sum(jnp.where(eye, row, 0.0), axis=1, keepdims=True)


class Far:
    def __init__(self, array, space=pltpu.VMEM):
        self.arrays = [pltpu.with_memory_space_constraint(array, pltpu.HBM)]
        self.pieces = array.shape[0] if array.ndim == 3 else 1
        self.buffer = space(array.shape, array.dtype)

    def copies(self, ref, buffer, sems):
        if self.pieces == 1:
            return [pltpu.make_async_copy(ref, buffer, sems.at[0])]
        return [
            pltpu.make_async_copy(ref.at[k], buffer.at[k], sems.at[k])
            for k in range(self.pieces)
        ]


class Fetched:
    def __init__(self, copies, ref):
        self.copies, self.ref, self.shape, self.done = copies, ref, ref.shape, 0

    def wait(self, upto=None):
        upto = len(self.copies) if upto is None else upto
        for k in range(self.done, upto):
            self.copies[k].wait()
        self.done = max(self.done, upto)
        return self.ref

    def all(self):
        return self.wait()[...]


def call(body, outs, scalars, operands, scratch=(), flops=0):
    flat, plan = [], []
    for one in operands:
        arrays = one.arrays if isinstance(one, Far) else one
        if not isinstance(arrays, (tuple, list)):
            arrays = [arrays]
        plan.append((one, len(flat), len(arrays)))
        flat.extend(arrays)
    fars = [one for one, _, _ in plan if isinstance(one, Far)]
    smem = pl.BlockSpec(memory_space=pltpu.SMEM)
    vmem = pl.BlockSpec(memory_space=pltpu.VMEM)
    specs = [smem] * len(scalars)
    for one, _, length in plan:
        specs += [pl.BlockSpec(memory_space=pl.ANY) if isinstance(one, Far) else vmem] * length

    def kernel(*refs):
        given, refs = refs[: len(scalars)], refs[len(scalars) :]
        arrays, refs = refs[: len(flat)], refs[len(flat) :]
        out, refs = refs[: len(outs)], refs[len(outs) :]
        mine, refs = refs[: len(scratch)], refs[len(scratch) :]
        buffers, sems = refs[: len(fars)], refs[len(fars) :]
        seen, at = [], 0
        for one, first, length in plan:
            if isinstance(one, Far):
                copies = one.copies(arrays[first], buffers[at], sems[at])
                for copy in copies:
                    copy.start()
                seen.append(Fetched(copies, buffers[at]))
                at += 1
            elif isinstance(one, (tuple, list)):
                seen.append(arrays[first : first + length])
            else:
                seen.append(arrays[first])
        body(*given, *seen, *out, *mine)

    outs = [o if isinstance(o, jax.ShapeDtypeStruct) else jax.ShapeDtypeStruct(o, F32) for o in outs]
    scratch = [o if isinstance(o, jax.ShapeDtypeStruct) else jax.ShapeDtypeStruct(o, F32) for o in scratch]
    return pl.pallas_call(
        kernel,
        out_shape=outs,
        in_specs=specs,
        out_specs=[vmem] * len(outs),
        scratch_shapes=[pltpu.VMEM(o.shape, o.dtype) for o in scratch]
        + [one.buffer for one in fars]
        + [pltpu.SemaphoreType.DMA((one.pieces,)) for one in fars],
        cost_estimate=pl.CostEstimate(
            flops=flops,
            bytes_accessed=sum(a.size * a.dtype.itemsize for a in flat),
            transcendentals=0,
        ),
        compiler_params=pltpu.CompilerParams(vmem_limit_bytes=GRANT),
    )(*scalars, *flat)


class Way:
    def __init__(self, chips):
        self.chips, self.power = chips, chips & (chips - 1) == 0

    def pairs(self, k):
        n = self.chips
        return [(i, i ^ k if self.power else (i + k) % n) for i in range(n)]

    def to(self, here, there):
        n = self.chips
        return there ^ here if self.power else lax.rem(there - here + n, n)

    def source(self, k):
        return k if self.power else (self.chips - k) % self.chips


def seats(way, cols):
    chip, core = lax.axis_index("chip"), lax.axis_index("core")
    first = lax.axis_index("row") * (2 * way.chips)
    found = []
    for k in range(cols.shape[0]):
        slot = jnp.maximum(cols[k] - first, 0)
        kind = jnp.where(lax.rem(slot, 2) == core, 0, way.chips)
        found.append(
            jnp.where(cols[k] >= 0, kind + way.to(chip, slot // 2), 2 * way.chips)
        )
    return found


def contributions(way, cols, pairs, panel, work, keep, send):
    chips = way.chips
    work[0 : 2 * chips] = jnp.zeros((2 * chips,) + work.shape[1:], F32)
    for seat, pair in zip(seats(way, cols), pairs):
        work[seat] = dot3(panel, pair(), NN)
    keep[...] = work[0:chips]
    send[...] = work[chips : 2 * chips]


def hold(gathered, held):
    for k, block in enumerate(gathered):
        high, low = split(block[...])
        rows = high.shape[0]
        held[k, 0:rows] = high
        held[k, rows : 2 * rows] = low
    held[len(gathered)] = jnp.zeros(held.shape[1:], BF16)


def off_diagonal(way, cols, pairs, held):
    rows = held.shape[1] // 2
    first = second = None
    for seat, pair in zip(seats(way, cols), pairs):
        both, (high, low) = held[seat], pair()
        one = lax.dot_general(both, high, NT, preferred_element_type=F32)
        two = lax.dot_general(both[:rows], low, NT, preferred_element_type=F32)
        first = one if first is None else first + one
        second = two if second is None else second + two
    return first[:rows] + (first[rows:] + second)


def held_pairs(split_tiles):
    return [
        functools.partial(lambda k: (split_tiles[0, k], split_tiles[1, k]), k)
        for k in range(split_tiles.shape[1])
    ]


def first_kernel(way, cols, panel, tiles, keep, send, split_tiles, work):
    cols = cols.wait()
    n = split_tiles.shape[1]

    def pair(k):
        if k in (0, (n + 1) // 2):
            tiles.wait(n if k else (n + 1) // 2)
        high, low = split(tiles.ref[k])
        split_tiles[0, k], split_tiles[1, k] = high, low
        return high, low

    pairs = [functools.partial(pair, k) for k in range(n)]
    contributions(way, cols, pairs, split(panel.all()), work, keep, send)


def diag_kernel(panel, diag, image):
    image[...] = dot_full(panel[...], diag[...], NT)


def off_kernel(way, cols, gathered, split_tiles, out, held):
    hold(gathered, held)
    out[...] = off_diagonal(way, cols, held_pairs(split_tiles), held)


def residual_kernel(
    way, cols, base, off, target, split_tiles, added, residual, keep, send, work
):
    total = base[...] + off[...]
    for block in added:
        total = total + block[...]
    rows, size = residual.shape
    chips = way.chips
    block = (lax.axis_index("row") * chips + lax.axis_index("chip")) * 2
    block = block + lax.axis_index("core")
    at = column_of((target[...] - block * size).astype(F32))
    unit = at == lax.broadcasted_iota(jnp.int32, (rows, size), 1).astype(F32)
    value = unit.astype(F32) - total
    residual[...] = value
    contributions(way, cols, held_pairs(split_tiles), split(value), work, keep, send)


def image_kernel(panel, base, off, added, image, half, sums):
    half[...] = off[...] + 0.5 * base[...]
    total = off[...] + base[...]
    for block in added:
        total = total + block[...]
    image[...] = total
    value = panel[...]
    found = jnp.concatenate(
        [row_sums(value * value), row_sums(value * total), row_sums(total * total)], 0
    )
    sums[...] = jnp.broadcast_to(found[None], sums.shape)


def steps(sums):
    totals = sums[0]
    for device in range(1, sums.shape[0]):
        totals = totals + sums[device]
    rr, rq, qq = totals[0:1], totals[1:2], totals[2:3]
    step = rr / rq
    norm = rr - 2.0 * step * rq + step * step * qq
    return column_of(step), column_of(norm / rr)


def newton_kernel(way, cols, gathered, diag, tiles, out, *more):
    *split_tiles, held = more
    rows = out.shape[0]
    for k, block in enumerate(gathered):
        value = block[...]
        high, rest = split(value)
        middle = value - high.astype(F32)
        held[k, 0:rows], held[k, rows : 2 * rows] = high, rest
        held[k, 2 * rows : 3 * rows] = (middle - rest.astype(F32)).astype(BF16)
    held[len(gathered)] = jnp.zeros(held.shape[1:], BF16)
    first = second = None
    work = [(seat, tiles[k]) for k, seat in enumerate(seats(way, cols))]
    for k, (seat, tile) in enumerate(work + [(0, None)]):
        three = held[seat]
        high, low = split(diag.all() * 0.5 if tile is None else tile)
        if tile is not None and split_tiles:
            split_tiles[0][0, k], split_tiles[0][1, k] = high, low
        one = lax.dot_general(three, high, NT, preferred_element_type=F32)
        two = lax.dot_general(three[: 2 * rows], low, NT, preferred_element_type=F32)
        first = one if first is None else first + one
        second = two if second is None else second + two
    small = first[2 * rows :] + second[rows:]
    out[...] = first[:rows] + (first[rows : 2 * rows] + second[:rows] + small)


def half_product(both, pair):
    rows = both.shape[0] // 2
    one = lax.dot_general(both, pair[0], NT, preferred_element_type=F32)
    two = lax.dot_general(both[:rows], pair[1], NT, preferred_element_type=F32)
    return one[:rows] + (one[rows:] + two)


def whole_pairs(tiles):
    return [
        functools.partial(lambda k: split(tiles[k]), k) for k in range(tiles.shape[0])
    ]


def halves_kernel(
    way, cols, images, tiles, newton_tiles, diag, newton_diag, half, newton, held
):
    hold(images, held)
    first = off_diagonal(way, cols, whole_pairs(tiles), held)
    second = off_diagonal(way, cols, held_pairs(newton_tiles), held)
    half[...] = first + half_product(held[0], split(diag.all() * 0.5))
    newton[...] = second + half_product(held[0], split(newton_diag.all() * 0.5))


def middle_kernel(
    parts_rows,
    parts_cols,
    sums,
    start,
    residual,
    image,
    half_residual,
    half_image,
    newton_start,
    newton_residual,
    newton_image,
    x_out,
    d_out,
    keep,
    send,
    order,
    blocks,
    pieces,
):
    step, ratio = steps(sums)
    count = d_out.shape[0]
    r, q = residual[...], image[...]
    x1 = start[...] + step * r
    r1 = r - step * q
    d1 = r1 + ratio * r
    grow = 1.0 + ratio
    x_out[...] = x1
    d_out[...] = d1
    half_d = grow * half_residual[...] - step * half_image[...]
    curvature = 2.0 * row_sums(d1 * half_d)
    norm = row_sums(r1 * r1)
    ux = newton_start[...] + step * newton_residual[...]
    ud = grow * newton_residual[...] - step * newton_image[...]
    hr, hc = count // parts_rows, count // parts_cols
    for r_index in range(parts_rows):
        for kind, pair in enumerate(((x1, ux), (d1, ud))):
            at = r_index * HALF + kind * hr
            for side in range(2):
                order[side, at : at + hr] = pair[side][
                    r_index * hr : (r_index + 1) * hr
                ]
        at = r_index * HALF + 2 * hr
        order[:, at : (r_index + 1) * HALF] = jnp.zeros(
            (2, HALF - 2 * hr, x1.shape[1]), F32
        )
    blocks[...] = dot_full(
        jnp.concatenate([x1, d1], axis=0), order[1], NT
    ) + dot_full(jnp.concatenate([ux, ud], axis=0), order[0], NT)
    depth = keep.shape[1]
    left = lax.broadcasted_iota(jnp.int32, (count, LANES), 1) < HALF
    pad = jnp.zeros((1, LANES - count), F32)
    wide = jnp.concatenate([curvature, pad], axis=1)
    norm = jnp.concatenate([norm, pad], axis=1)
    line = lax.broadcasted_iota(jnp.int32, (depth, LANES), 0)
    wide = jnp.where(line == hc, wide, norm)
    spot = (line == hc) | (line == hc + 1)
    first_core = lax.axis_index("core") == 0
    for r_index in range(parts_rows):
        lanes = slice(r_index // 2 * LANES, (r_index // 2 + 1) * LANES)
        top, bottom = blocks[0:count, lanes], blocks[count : 2 * count, lanes]
        if r_index % 2:
            top = pltpu.roll(top, HALF, 1)
        else:
            bottom = pltpu.roll(bottom, HALF, 1)
        pieces[r_index, 0:count] = jnp.where(left, top, bottom)
        for pair in range(parts_cols // 2):
            one, two = (
                jnp.where(spot, wide, pieces[r_index, c * hc : c * hc + depth])
                for c in (2 * pair, 2 * pair + 1)
            )
            at = r_index * (parts_cols // 2) + pair
            keep[at] = jnp.where(first_core, one, two)
            send[at] = jnp.where(first_core, two, one)


def last_kernel(parts_rows, parts_cols, received, x1, d1, x_out, hessian):
    total = received[0]
    for device in range(1, received.shape[0]):
        total = total + received[device]
    count = x1.shape[0]
    hr, hc = count // parts_rows, count // parts_cols
    step = total[hc + 1 : hc + 2, 0:count] / total[hc : hc + 1, 0:count]
    step_col = column_of(step)
    x_out[...] = x1[...] + step_col * d1[...]
    row_at = lax.axis_index("row") * hr
    col_at = (lax.axis_index("chip") * 2 + lax.axis_index("core")) * hc
    wanted = lax.broadcasted_iota(jnp.int32, (count, hr), 0) == row_at + (
        lax.broadcasted_iota(jnp.int32, (count, hr), 1)
    )
    of_rows = jnp.sum(jnp.where(wanted, step_col, 0.0), axis=0, keepdims=True)
    wanted = lax.broadcasted_iota(jnp.int32, (hc, count), 1) == col_at + (
        lax.broadcasted_iota(jnp.int32, (hc, count), 0)
    )
    of_cols = jnp.sum(jnp.where(wanted, step, 0.0), axis=1, keepdims=True)
    xx = total[0:hc, 0:hr]
    dx = total[0:hc, hr : 2 * hr]
    xd = total[0:hc, HALF : HALF + hr]
    dd = total[0:hc, HALF + hr : HALF + 2 * hr]
    hessian[...] = xx + of_rows * dx + of_cols * (xd + of_rows * dd)


def on_device(
    precision_diag,
    precision_pairs,
    pattern_cols,
    newton_diag,
    newton_pairs,
    warm_start,
    target_rows,
):
    groups = lax.axis_size("row")
    chips = lax.axis_size("chip")
    columns = chips * 2
    count, size = warm_start.shape[1:]
    n = precision_pairs.shape[1]
    cols = pattern_cols[0]
    target = target_rows[None]
    tiles, diag = precision_pairs[0], precision_diag[0]
    ntiles, ndiag = newton_pairs[0], newton_diag[0]
    panel = (count, size)
    stack = (chips, count, size)
    swap = [(0, 1), (1, 0)]
    way = Way(chips)
    unit = 2 * count * size * size * 3
    parts = jax.ShapeDtypeStruct((2, n, size, size), BF16)
    work = (2 * chips + 1,) + panel
    held = jax.ShapeDtypeStruct((2 * chips + 1, 2 * count, size), BF16)

    def gather(value):
        same = [value] + [None] * (chips - 1)
        for k in range(1, chips):
            same[way.source(k)] = lax.ppermute(value, "chip", way.pairs(k))
        return same

    def forward(same):
        return list(same) + [lax.ppermute(block, "core", swap) for block in same]

    def scatter(keep, send):
        received = lax.ppermute(send, "core", swap)
        sums = [keep[k] + received[k] for k in range(chips)]
        added = [sums[0]]
        for k in range(1, chips):
            added.append(lax.ppermute(sums[k], "chip", way.pairs(k)))
        return added

    start = warm_start[0]
    starts = gather(start)
    keep, send, split_tiles = call(
        functools.partial(first_kernel, way),
        [stack, stack, parts],
        [],
        [Far(cols, pltpu.SMEM), Far(start), Far(tiles)],
        scratch=[work],
        flops=n * unit,
    )
    added = scatter(keep, send)
    starts = forward(starts)
    (base,) = call(diag_kernel, [panel], [], [start, diag], flops=2 * unit)

    def off_half(gathered):
        return call(
            functools.partial(off_kernel, way),
            [panel],
            [cols],
            [gathered, split_tiles],
            scratch=[held],
            flops=n * unit,
        )[0]

    residual, keep, send = call(
        functools.partial(residual_kernel, way),
        [panel, stack, stack],
        [cols],
        [base, off_half(starts), target, split_tiles, added],
        scratch=[work],
        flops=n * unit,
    )
    residuals = gather(residual)
    added = scatter(keep, send)
    residuals = forward(residuals)
    (base,) = call(diag_kernel, [panel], [], [residual, diag], flops=2 * unit)

    def newton_half(gathered, phase):
        return call(
            functools.partial(newton_kernel, way),
            [panel, parts][: phase + 1],
            [cols],
            [gathered, Far(ndiag), ntiles],
            scratch=[
                jax.ShapeDtypeStruct((2 * chips + 1, 3 * count, size), BF16)
            ],
            flops=2 * n * unit,
        )

    (newton_start,) = newton_half(starts, 0)
    newton_residual, newton_tiles = newton_half(residuals, 1)
    image, half_residual, sums = call(
        image_kernel,
        [panel, panel, (groups * columns, 3, count)],
        [],
        [residual, base, off_half(residuals), added],
        flops=unit // 10,
    )
    images = gather(image)
    sums = lax.all_to_all(sums, ALL, 0, 0, tiled=True)
    images = forward(images)
    hr, hc = count // groups, count // columns
    depth = -(-(hc + 2) // 8) * 8
    share = (groups * chips, depth, LANES)
    half_image, newton_image = call(
        functools.partial(halves_kernel, way),
        [panel, panel],
        [cols],
        [images, tiles, newton_tiles, Far(diag), Far(ndiag)],
        scratch=[held],
        flops=2 * n * unit,
    )
    x1, d1, keep, send = call(
        functools.partial(middle_kernel, groups, columns),
        [panel, panel, share, share],
        [],
        [
            sums,
            start,
            residual,
            image,
            half_residual,
            half_image,
            newton_start,
            newton_residual,
            newton_image,
        ],
        scratch=[
            (2, groups * HALF, size),
            (2 * count, groups * HALF),
            (groups, count + depth, LANES),
        ],
        flops=n * unit,
    )
    received = lax.ppermute(send, "core", swap)
    received = lax.all_to_all(keep + received, ("row", "chip"), 0, 0, tiled=True)
    solved, hessian = call(
        functools.partial(last_kernel, groups, columns),
        [panel, (hc, hr)],
        [],
        [received, x1, d1],
        flops=unit // 100,
    )
    return solved[None], hessian.T


def solution(mesh):
    rows, columns = mesh.devices.shape
    fine = Mesh(mesh.devices.reshape(rows, columns // 2, 2), ALL)
    placed = (
        P(ALL, None, None),
        P(ALL, None, None, None),
        P(ALL, None),
        P(ALL, None, None),
        P(ALL, None, None, None),
        P(ALL, None, None),
        P(),
    )
    return jax.shard_map(
        on_device,
        mesh=fine,
        in_specs=placed,
        out_specs=(P(ALL, None, None), P("row", ("chip", "core"))),
        check_vma=False,
    )
```

```python
import functools

import jax
import jax.numpy as jnp
from jax import lax
from jax.experimental import pallas as pl
from jax.experimental.pallas import tpu as pltpu
from jax.sharding import Mesh, PartitionSpec as P


F32 = jnp.float32
BF16 = jnp.bfloat16
ALL = ("row", "chip", "core")
GRANT = 24 << 20
LANES = 128
HALF = 64

NT = (((1,), (1,)), ((), ()))
NN = (((1,), (0,)), ((), ()))


def split(value):
    high = value.astype(BF16)
    low = (value - high.astype(F32)).astype(BF16)
    return high, low


def dot3(left, right, dims):
    rows = left[0].shape[0]
    both = jnp.concatenate(left, axis=0)
    first = lax.dot_general(both, right[0], dims, preferred_element_type=F32)
    second = lax.dot_general(left[0], right[1], dims, preferred_element_type=F32)
    return first[:rows] + first[rows:] + second


def dot_full(left, right, dims):
    return lax.dot_general(
        left, right, dims, precision=lax.Precision.HIGHEST, preferred_element_type=F32
    )


def row_sums(product):
    return dot_full(jnp.ones((8, product.shape[1]), F32), product, NT)[0:1]


def column_of(row):
    n = row.shape[1]
    eye = lax.broadcasted_iota(jnp.int32, (n, n), 0) == lax.broadcasted_iota(
        jnp.int32, (n, n), 1
    )
    return jnp.sum(jnp.where(eye, row, 0.0), axis=1, keepdims=True)


class Far:
    def __init__(self, array, space=pltpu.VMEM):
        self.arrays = [pltpu.with_memory_space_constraint(array, pltpu.HBM)]
        self.pieces = array.shape[0] if array.ndim == 3 else 1
        self.buffer = space(array.shape, array.dtype)

    def copies(self, ref, buffer, sems):
        if self.pieces == 1:
            return [pltpu.make_async_copy(ref, buffer, sems.at[0])]
        return [
            pltpu.make_async_copy(ref.at[k], buffer.at[k], sems.at[k])
            for k in range(self.pieces)
        ]


class Fetched:
    def __init__(self, copies, ref):
        self.copies, self.ref, self.shape, self.done = copies, ref, ref.shape, 0

    def wait(self, upto=None):
        upto = len(self.copies) if upto is None else upto
        for k in range(self.done, upto):
            self.copies[k].wait()
        self.done = max(self.done, upto)
        return self.ref

    def all(self):
        return self.wait()[...]


def call(body, outs, scalars, operands, scratch=(), flops=0):
    flat, plan = [], []
    for one in operands:
        arrays = one.arrays if isinstance(one, Far) else one
        if not isinstance(arrays, (tuple, list)):
            arrays = [arrays]
        plan.append((one, len(flat), len(arrays)))
        flat.extend(arrays)
    fars = [one for one, _, _ in plan if isinstance(one, Far)]
    smem = pl.BlockSpec(memory_space=pltpu.SMEM)
    vmem = pl.BlockSpec(memory_space=pltpu.VMEM)
    specs = [smem] * len(scalars)
    for one, _, length in plan:
        specs += [pl.BlockSpec(memory_space=pl.ANY) if isinstance(one, Far) else vmem] * length

    def kernel(*refs):
        given, refs = refs[: len(scalars)], refs[len(scalars) :]
        arrays, refs = refs[: len(flat)], refs[len(flat) :]
        out, refs = refs[: len(outs)], refs[len(outs) :]
        mine, refs = refs[: len(scratch)], refs[len(scratch) :]
        buffers, sems = refs[: len(fars)], refs[len(fars) :]
        seen, at = [], 0
        for one, first, length in plan:
            if isinstance(one, Far):
                copies = one.copies(arrays[first], buffers[at], sems[at])
                for copy in copies:
                    copy.start()
                seen.append(Fetched(copies, buffers[at]))
                at += 1
            elif isinstance(one, (tuple, list)):
                seen.append(arrays[first : first + length])
            else:
                seen.append(arrays[first])
        body(*given, *seen, *out, *mine)

    outs = [o if isinstance(o, jax.ShapeDtypeStruct) else jax.ShapeDtypeStruct(o, F32) for o in outs]
    scratch = [o if isinstance(o, jax.ShapeDtypeStruct) else jax.ShapeDtypeStruct(o, F32) for o in scratch]
    return pl.pallas_call(
        kernel,
        out_shape=outs,
        in_specs=specs,
        out_specs=[vmem] * len(outs),
        scratch_shapes=[pltpu.VMEM(o.shape, o.dtype) for o in scratch]
        + [one.buffer for one in fars]
        + [pltpu.SemaphoreType.DMA((one.pieces,)) for one in fars],
        cost_estimate=pl.CostEstimate(
            flops=flops,
            bytes_accessed=sum(a.size * a.dtype.itemsize for a in flat),
            transcendentals=0,
        ),
        compiler_params=pltpu.CompilerParams(vmem_limit_bytes=GRANT),
    )(*scalars, *flat)


class Way:
    def __init__(self, chips):
        self.chips, self.power = chips, chips & (chips - 1) == 0

    def pairs(self, k):
        n = self.chips
        return [(i, i ^ k if self.power else (i + k) % n) for i in range(n)]

    def to(self, here, there):
        n = self.chips
        return there ^ here if self.power else lax.rem(there - here + n, n)

    def source(self, k):
        return k if self.power else (self.chips - k) % self.chips


def seats(way, cols):
    chip, core = lax.axis_index("chip"), lax.axis_index("core")
    first = lax.axis_index("row") * (2 * way.chips)
    found = []
    for k in range(cols.shape[0]):
        slot = jnp.maximum(cols[k] - first, 0)
        kind = jnp.where(lax.rem(slot, 2) == core, 0, way.chips)
        found.append(
            jnp.where(cols[k] >= 0, kind + way.to(chip, slot // 2), 2 * way.chips)
        )
    return found


def contributions(way, cols, pairs, panel, work, keep, send):
    chips = way.chips
    work[0 : 2 * chips] = jnp.zeros((2 * chips,) + work.shape[1:], F32)
    for seat, pair in zip(seats(way, cols), pairs):
        work[seat] = dot3(panel, pair(), NN)
    keep[...] = work[0:chips]
    send[...] = work[chips : 2 * chips]


def hold(gathered, held):
    for k, block in enumerate(gathered):
        high, low = split(block[...])
        rows = high.shape[0]
        held[k, 0:rows] = high
        held[k, rows : 2 * rows] = low
    held[len(gathered)] = jnp.zeros(held.shape[1:], BF16)


def off_diagonal(way, cols, pairs, held):
    rows = held.shape[1] // 2
    first = second = None
    for seat, pair in zip(seats(way, cols), pairs):
        both, (high, low) = held[seat], pair()
        one = lax.dot_general(both, high, NT, preferred_element_type=F32)
        two = lax.dot_general(both[:rows], low, NT, preferred_element_type=F32)
        first = one if first is None else first + one
        second = two if second is None else second + two
    return first[:rows] + (first[rows:] + second)


def held_pairs(split_tiles):
    return [
        functools.partial(lambda k: (split_tiles[0, k], split_tiles[1, k]), k)
        for k in range(split_tiles.shape[1])
    ]


def first_kernel(way, cols, panel, tiles, keep, send, split_tiles, work):
    cols = cols.wait()
    n = split_tiles.shape[1]

    def pair(k):
        if k in (0, (n + 1) // 2):
            tiles.wait(n if k else (n + 1) // 2)
        high, low = split(tiles.ref[k])
        split_tiles[0, k], split_tiles[1, k] = high, low
        return high, low

    pairs = [functools.partial(pair, k) for k in range(n)]
    contributions(way, cols, pairs, split(panel.all()), work, keep, send)


def diag_kernel(panel, diag, image):
    image[...] = dot_full(panel[...], diag[...], NT)


def off_kernel(way, cols, gathered, split_tiles, out, held):
    hold(gathered, held)
    out[...] = off_diagonal(way, cols, held_pairs(split_tiles), held)


def residual_kernel(
    way, cols, base, off, target, split_tiles, added, residual, keep, send, work
):
    total = base[...] + off[...]
    for block in added:
        total = total + block[...]
    rows, size = residual.shape
    chips = way.chips
    block = (lax.axis_index("row") * chips + lax.axis_index("chip")) * 2
    block = block + lax.axis_index("core")
    at = column_of((target[...] - block * size).astype(F32))
    unit = at == lax.broadcasted_iota(jnp.int32, (rows, size), 1).astype(F32)
    value = unit.astype(F32) - total
    residual[...] = value
    contributions(way, cols, held_pairs(split_tiles), split(value), work, keep, send)


def image_kernel(panel, base, off, added, image, half, sums):
    half[...] = off[...] + 0.5 * base[...]
    total = off[...] + base[...]
    for block in added:
        total = total + block[...]
    image[...] = total
    value = panel[...]
    found = jnp.concatenate(
        [row_sums(value * value), row_sums(value * total), row_sums(total * total)], 0
    )
    sums[...] = jnp.broadcast_to(found[None], sums.shape)


def steps(sums):
    totals = sums[0]
    for device in range(1, sums.shape[0]):
        totals = totals + sums[device]
    rr, rq, qq = totals[0:1], totals[1:2], totals[2:3]
    step = rr / rq
    norm = rr - 2.0 * step * rq + step * step * qq
    return column_of(step), column_of(norm / rr)


def newton_kernel(way, cols, gathered, diag, tiles, out, *more):
    *split_tiles, held = more
    rows = out.shape[0]
    for k, block in enumerate(gathered):
        held[k, 0:rows], held[k, rows : 2 * rows] = split(block[...])
    held[len(gathered)] = jnp.zeros(held.shape[1:], BF16)
    first = second = None
    work = [(seat, tiles[k]) for k, seat in enumerate(seats(way, cols))]
    for k, (seat, tile) in enumerate(work + [(0, None)]):
        three = held[seat]
        high, low = split(diag.all() * 0.5 if tile is None else tile)
        if tile is not None and split_tiles:
            split_tiles[0][0, k], split_tiles[0][1, k] = high, low
        one = lax.dot_general(three, high, NT, preferred_element_type=F32)
        two = lax.dot_general(three[: 2 * rows], low, NT, preferred_element_type=F32)
        first = one if first is None else first + one
        second = two if second is None else second + two
    out[...] = first[:rows] + (first[rows:] + second[:rows] + second[rows:])


def half_product(both, pair):
    rows = both.shape[0] // 2
    one = lax.dot_general(both, pair[0], NT, preferred_element_type=F32)
    two = lax.dot_general(both[:rows], pair[1], NT, preferred_element_type=F32)
    return one[:rows] + (one[rows:] + two)


def whole_pairs(tiles):
    return [
        functools.partial(lambda k: split(tiles[k]), k) for k in range(tiles.shape[0])
    ]


def halves_kernel(
    way, cols, images, tiles, newton_tiles, diag, newton_diag, half, newton, held
):
    hold(images, held)
    first = off_diagonal(way, cols, whole_pairs(tiles), held)
    second = off_diagonal(way, cols, held_pairs(newton_tiles), held)
    half[...] = first + half_product(held[0], split(diag.all() * 0.5))
    newton[...] = second + half_product(held[0], split(newton_diag.all() * 0.5))


def middle_kernel(
    parts_rows,
    parts_cols,
    sums,
    start,
    residual,
    image,
    half_residual,
    half_image,
    newton_start,
    newton_residual,
    newton_image,
    x_out,
    d_out,
    keep,
    send,
    order,
    blocks,
    pieces,
):
    step, ratio = steps(sums)
    count = d_out.shape[0]
    r, q = residual[...], image[...]
    x1 = start[...] + step * r
    r1 = r - step * q
    d1 = r1 + ratio * r
    grow = 1.0 + ratio
    x_out[...] = x1
    d_out[...] = d1
    half_d = grow * half_residual[...] - step * half_image[...]
    curvature = 2.0 * row_sums(d1 * half_d)
    norm = row_sums(r1 * r1)
    ux = newton_start[...] + step * newton_residual[...]
    ud = grow * newton_residual[...] - step * newton_image[...]
    hr, hc = count // parts_rows, count // parts_cols
    for r_index in range(parts_rows):
        for kind, pair in enumerate(((x1, ux), (d1, ud))):
            at = r_index * HALF + kind * hr
            for side in range(2):
                order[side, at : at + hr] = pair[side][
                    r_index * hr : (r_index + 1) * hr
                ]
        at = r_index * HALF + 2 * hr
        order[:, at : (r_index + 1) * HALF] = jnp.zeros(
            (2, HALF - 2 * hr, x1.shape[1]), F32
        )
    blocks[...] = dot_full(
        jnp.concatenate([x1, d1], axis=0), order[1], NT
    ) + dot_full(jnp.concatenate([ux, ud], axis=0), order[0], NT)
    depth = keep.shape[1]
    left = lax.broadcasted_iota(jnp.int32, (count, LANES), 1) < HALF
    pad = jnp.zeros((1, LANES - count), F32)
    wide = jnp.concatenate([curvature, pad], axis=1)
    norm = jnp.concatenate([norm, pad], axis=1)
    line = lax.broadcasted_iota(jnp.int32, (depth, LANES), 0)
    wide = jnp.where(line == hc, wide, norm)
    spot = (line == hc) | (line == hc + 1)
    first_core = lax.axis_index("core") == 0
    for r_index in range(parts_rows):
        lanes = slice(r_index // 2 * LANES, (r_index // 2 + 1) * LANES)
        top, bottom = blocks[0:count, lanes], blocks[count : 2 * count, lanes]
        if r_index % 2:
            top = pltpu.roll(top, HALF, 1)
        else:
            bottom = pltpu.roll(bottom, HALF, 1)
        pieces[r_index, 0:count] = jnp.where(left, top, bottom)
        for pair in range(parts_cols // 2):
            one, two = (
                jnp.where(spot, wide, pieces[r_index, c * hc : c * hc + depth])
                for c in (2 * pair, 2 * pair + 1)
            )
            at = r_index * (parts_cols // 2) + pair
            keep[at] = jnp.where(first_core, one, two)
            send[at] = jnp.where(first_core, two, one)


def last_kernel(parts_rows, parts_cols, received, x1, d1, x_out, hessian):
    total = received[0]
    for device in range(1, received.shape[0]):
        total = total + received[device]
    count = x1.shape[0]
    hr, hc = count // parts_rows, count // parts_cols
    step = total[hc + 1 : hc + 2, 0:count] / total[hc : hc + 1, 0:count]
    step_col = column_of(step)
    x_out[...] = x1[...] + step_col * d1[...]
    row_at = lax.axis_index("row") * hr
    col_at = (lax.axis_index("chip") * 2 + lax.axis_index("core")) * hc
    wanted = lax.broadcasted_iota(jnp.int32, (count, hr), 0) == row_at + (
        lax.broadcasted_iota(jnp.int32, (count, hr), 1)
    )
    of_rows = jnp.sum(jnp.where(wanted, step_col, 0.0), axis=0, keepdims=True)
    wanted = lax.broadcasted_iota(jnp.int32, (hc, count), 1) == col_at + (
        lax.broadcasted_iota(jnp.int32, (hc, count), 0)
    )
    of_cols = jnp.sum(jnp.where(wanted, step, 0.0), axis=1, keepdims=True)
    xx = total[0:hc, 0:hr]
    dx = total[0:hc, hr : 2 * hr]
    xd = total[0:hc, HALF : HALF + hr]
    dd = total[0:hc, HALF + hr : HALF + 2 * hr]
    hessian[...] = xx + of_rows * dx + of_cols * (xd + of_rows * dd)


def on_device(
    precision_diag,
    precision_pairs,
    pattern_cols,
    newton_diag,
    newton_pairs,
    warm_start,
    target_rows,
):
    groups = lax.axis_size("row")
    chips = lax.axis_size("chip")
    columns = chips * 2
    count, size = warm_start.shape[1:]
    n = precision_pairs.shape[1]
    cols = pattern_cols[0]
    target = target_rows[None]
    tiles, diag = precision_pairs[0], precision_diag[0]
    ntiles, ndiag = newton_pairs[0], newton_diag[0]
    panel = (count, size)
    stack = (chips, count, size)
    swap = [(0, 1), (1, 0)]
    way = Way(chips)
    unit = 2 * count * size * size * 3
    parts = jax.ShapeDtypeStruct((2, n, size, size), BF16)
    work = (2 * chips + 1,) + panel
    held = jax.ShapeDtypeStruct((2 * chips + 1, 2 * count, size), BF16)

    def gather(value):
        same = [value] + [None] * (chips - 1)
        for k in range(1, chips):
            same[way.source(k)] = lax.ppermute(value, "chip", way.pairs(k))
        return same

    def forward(same):
        return list(same) + [lax.ppermute(block, "core", swap) for block in same]

    def scatter(keep, send):
        received = lax.ppermute(send, "core", swap)
        sums = [keep[k] + received[k] for k in range(chips)]
        added = [sums[0]]
        for k in range(1, chips):
            added.append(lax.ppermute(sums[k], "chip", way.pairs(k)))
        return added

    start = warm_start[0]
    starts = gather(start)
    keep, send, split_tiles = call(
        functools.partial(first_kernel, way),
        [stack, stack, parts],
        [],
        [Far(cols, pltpu.SMEM), Far(start), Far(tiles)],
        scratch=[work],
        flops=n * unit,
    )
    added = scatter(keep, send)
    starts = forward(starts)
    (base,) = call(diag_kernel, [panel], [], [start, diag], flops=2 * unit)

    def off_half(gathered):
        return call(
            functools.partial(off_kernel, way),
            [panel],
            [cols],
            [gathered, split_tiles],
            scratch=[held],
            flops=n * unit,
        )[0]

    residual, keep, send = call(
        functools.partial(residual_kernel, way),
        [panel, stack, stack],
        [cols],
        [base, off_half(starts), target, split_tiles, added],
        scratch=[work],
        flops=n * unit,
    )
    residuals = gather(residual)
    added = scatter(keep, send)
    residuals = forward(residuals)
    (base,) = call(diag_kernel, [panel], [], [residual, diag], flops=2 * unit)

    def newton_half(gathered, phase):
        return call(
            functools.partial(newton_kernel, way),
            [panel, parts][: phase + 1],
            [cols],
            [gathered, Far(ndiag), ntiles],
            scratch=[
                held
            ],
            flops=2 * n * unit,
        )

    (newton_start,) = newton_half(starts, 0)
    newton_residual, newton_tiles = newton_half(residuals, 1)
    image, half_residual, sums = call(
        image_kernel,
        [panel, panel, (groups * columns, 3, count)],
        [],
        [residual, base, off_half(residuals), added],
        flops=unit // 10,
    )
    images = gather(image)
    sums = lax.all_to_all(sums, ALL, 0, 0, tiled=True)
    images = forward(images)
    hr, hc = count // groups, count // columns
    depth = -(-(hc + 2) // 8) * 8
    share = (groups * chips, depth, LANES)
    half_image, newton_image = call(
        functools.partial(halves_kernel, way),
        [panel, panel],
        [cols],
        [images, tiles, newton_tiles, Far(diag), Far(ndiag)],
        scratch=[held],
        flops=2 * n * unit,
    )
    x1, d1, keep, send = call(
        functools.partial(middle_kernel, groups, columns),
        [panel, panel, share, share],
        [],
        [
            sums,
            start,
            residual,
            image,
            half_residual,
            half_image,
            newton_start,
            newton_residual,
            newton_image,
        ],
        scratch=[
            (2, groups * HALF, size),
            (2 * count, groups * HALF),
            (groups, count + depth, LANES),
        ],
        flops=n * unit,
    )
    received = lax.ppermute(send, "core", swap)
    received = lax.all_to_all(keep + received, ("row", "chip"), 0, 0, tiled=True)
    solved, hessian = call(
        functools.partial(last_kernel, groups, columns),
        [panel, (hc, hr)],
        [],
        [received, x1, d1],
        flops=unit // 100,
    )
    return solved[None], hessian.T


def solution(mesh):
    rows, columns = mesh.devices.shape
    fine = Mesh(mesh.devices.reshape(rows, columns // 2, 2), ALL)
    placed = (
        P(ALL, None, None),
        P(ALL, None, None, None),
        P(ALL, None),
        P(ALL, None, None),
        P(ALL, None, None, None),
        P(ALL, None, None),
        P(),
    )
    return jax.shard_map(
        on_device,
        mesh=fine,
        in_specs=placed,
        out_specs=(P(ALL, None, None), P("row", ("chip", "core"))),
        check_vma=False,
    )
```
